32 devices in a mesh: dp: 8 (over y, x, core), tensor: 4 (over z).
Axes of the slice: x: 2, y: 2, z: 4, core: 2. Of those that a mesh axis runs over, the one named last changes fastest.
Arguments:
- block_input: float32 [4096, 2048], P(('dp', 'tensor'))
- out_grad: float32 [4096, 2048], P(('dp', 'tensor')), may hold values from -6 to 6
- segments: int32 [4096], P('dp'), may hold values from 0 to 4, never falling along the last dimension, each value on 1 to 2000 neighbouring positions
- routes: int32 [4096, 6], P('dp'), may hold values from 0 to 15, all different within a row; in each aligned block of 128 rows (0 to 127, 128 to 255, ...) at most 72 rows name the same one
- route_weight: float32 [4096, 6], P('dp'), may hold values from 0.1 to 0.6
- norm_attn: bfloat16 [2048], P(('dp', 'tensor')), may hold values from 0.5 to 1.5
- query_down: bfloat16 [2048, 1536], P(('dp', 'tensor')), may hold values from -0.125 to 0.125
- query_norm: bfloat16 [1536], P(('dp', 'tensor')), may hold values from 0.5 to 1.5
- query_up: bfloat16 [1536, 3072], P('dp', 'tensor'), may hold values from -0.15625 to 0.15625
- latent_down: bfloat16 [2048, 576], P(('dp', 'tensor')), may hold values from -0.125 to 0.125
- latent_norm: bfloat16 [512], P(('dp', 'tensor')), may hold values from 0.5 to 1.5
- latent_up: bfloat16 [512, 4096], P('dp', 'tensor'), may hold values from -0.25 to 0.25
- out_proj: bfloat16 [2048, 2048], P('dp', 'tensor'), may hold values from -1 to 1
- norm_ffn: bfloat16 [2048], P(('dp', 'tensor')), may hold values from 0.5 to 1.5
- shared_gate: bfloat16 [2048, 2816], P('dp', 'tensor'), may hold values from -0.125 to 0.125
- shared_up: bfloat16 [2048, 2816], P('dp', 'tensor'), may hold values from -0.125 to 0.125
- shared_down: bfloat16 [2048, 2816], P('dp', 'tensor'), may hold values from -0.109375 to 0.109375
- expert_gate: bfloat16 [16, 2048, 1408], P('dp', None, 'tensor'), may hold values from -0.125 to 0.125
- expert_up: bfloat16 [16, 2048, 1408], P('dp', None, 'tensor'), may hold values from -0.125 to 0.125
- expert_down: bfloat16 [16, 2048, 1408], P('dp', None, 'tensor'), may hold values from -0.15625 to 0.15625
Outputs:
- block_output: float32 [4096, 2048], P(('dp', 'tensor'))
- input_grad: float32 [4096, 2048], P(('dp', 'tensor'))
- grad_norm_attn: float32 [2048], P(('dp', 'tensor'))
- grad_query_down: float32 [2048, 1536], P(('dp', 'tensor'))
- grad_query_norm: float32 [1536], P(('dp', 'tensor'))
- grad_query_up: float32 [1536, 3072], P('dp', 'tensor')
- grad_latent_down: float32 [2048, 576], P(('dp', 'tensor'))
- grad_latent_norm: float32 [512], P(('dp', 'tensor'))
- grad_latent_up: float32 [512, 4096], P('dp', 'tensor')
- grad_out_proj: float32 [2048, 2048], P('dp', 'tensor')
- grad_norm_ffn: float32 [2048], P(('dp', 'tensor'))
- grad_shared_gate: float32 [2048, 2816], P('dp', 'tensor')
- grad_shared_up: float32 [2048, 2816], P('dp', 'tensor')
- grad_shared_down: float32 [2048, 2816], P('dp', 'tensor')
- grad_expert_gate: float32 [16, 2048, 1408], P('dp', None, 'tensor')
- grad_expert_up: float32 [16, 2048, 1408], P('dp', None, 'tensor')
- grad_expert_down: float32 [16, 2048, 1408], P('dp', None, 'tensor')
The draws below stay inside these ranges and needn't reach their ends.
Inputs may be any that keep to these rules, and one draw needn't show every extreme that they name: `segments`: segment numbers never fall along the tokens; a segment holds at most 2000 tokens and at most half of all tokens. `routes`: each row names 6 different experts. In each aligned block of 128 rows no expert is named by more than 72 rows, a bound that some block reaches.
All inputs are finite; a program needn't handle non-finite values.
Results may differ from the reference program's by a relative error of at most 0.024.
Values may be sent and summed in bfloat16 or wider, within the bound.
No kernel may reach another device: no remote copies, remote signals or barrier semaphores. Data moves between devices by JAX's collectives and lax.ppermute only.
A program may use at most 384 MiB of HBM per device.

```python
import math
import jax
import jax.numpy as jnp
import numpy as np
from jax import lax

D = 2048
HEADS = 16
NOPE = 128
ROPE = 64
VDIM = 128
QRANK = 1536
KVRANK = 512
FF = 1408
SHARED = 2816
TOPK = 6
SEQ = 512
EXPERTS = 16
ROWS = 128
CAP = 72
TOKENS = 4096
N_TENSOR = 4


def draw_block_input(key, part):
    first, second, third = jax.random.split(key, 3)
    row_scale = jnp.exp(jax.random.uniform(second, (TOKENS, 1), jnp.float32, -1.2, 1.2))
    column_scale = jnp.exp(jax.random.uniform(third, (1, D), jnp.float32, -0.6, 0.6))
    base = jax.random.normal(first, (TOKENS, D), jnp.float32)
    return (base * row_scale * column_scale).astype(jnp.float32)


def level_of(stream_key, extent, cuts, smallest, high):
    level, own = 1.0, jax.random.fold_in(stream_key, 6)
    for dim, blocks in cuts:
        steps = jnp.exp(jax.random.uniform(jax.random.fold_in(own, dim), (blocks,), jnp.float32, smallest / len(cuts), high / len(cuts)))
        level = level * jnp.repeat(steps, extent[dim] // blocks).reshape([-1 if axis == dim else 1 for axis in range(len(extent))])
    return level


def split_up(count, total, most, lean):
    portions = [(1 << 20) // math.isqrt(grade ** lean) + 1 for grade in range(2, count + 1)]
    rest, holding = total - most - (count - 1), [1] * (count - 1)
    while rest > 0:
        movable = [i for i in range(count - 1) if holding[i] < most]
        pool, left = sum([portions[i] for i in movable]), rest
        for i in movable:
            extra = min(most - holding[i], max(1, left * portions[i] // pool), rest)
            holding[i] = holding[i] + extra
            rest = rest - extra
    return np.array([most] + holding)


def uneven_parts(stream_key, count, total, bound, skew):
    if count == 2:
        one = jax.random.randint(stream_key, (), max(1, total - bound), min(bound, total - 1) + 1)
        return jnp.stack([one, total - one])
    tallies = jnp.asarray(split_up(count, total, bound, skew), jnp.int32)
    twos = (count - 1) // 2
    giver, taker = tallies[1:1 + 2 * twos:2], tallies[2:2 + 2 * twos:2]
    room = jnp.minimum(giver - 1, bound - taker)
    moved = jax.random.randint(jax.random.fold_in(stream_key, 1), (twos,), 0, 1 << 20) % (room + 1)
    tallies = tallies.at[1:1 + 2 * twos:2].set(giver - moved).at[2:2 + 2 * twos:2].set(taker + moved)
    return tallies[jax.random.permutation(jax.random.fold_in(stream_key, 2), count)]


def routed_block(rng, own, number, rows, amount, top, most, lean):
    sequence = jax.random.permutation(rng, amount)
    heavy_load, ordinary = load_shares(amount, rows * top, most, lean, True), load_shares(amount, rows * top, most, lean, False)
    places = jnp.arange(amount)

    def named(sizes, offset_by):
        used = int((sizes > 0).sum())
        fixed = max(1, used // 4)
        passed = fixed + (places - fixed + offset_by * (used - fixed)) % max(1, amount - fixed)
        return jnp.zeros((amount,), jnp.int32).at[sequence[jnp.where(places < fixed, places, passed)]].set(jnp.asarray(sizes, jnp.int32))

    sizes = jnp.where(number % 4 == 0, named(heavy_load, number // 4), named(ordinary, number - number // 4 - 1))
    mixed = jax.random.permutation(jax.random.fold_in(own, 3), amount)
    donor, receiver = mixed[0:amount // 2 * 2:2], mixed[1:amount // 2 * 2:2]
    margin = jnp.minimum(sizes[donor] - 1, most - sizes[receiver]) // 2
    margin = jnp.where((donor == sequence[0]) | (receiver == sequence[0]) | (sizes[receiver] == 0), 0, jnp.maximum(margin, 0))
    passed = jax.random.randint(jax.random.fold_in(own, 4), (amount // 2,), 0, 1 << 20) % (margin + 1)
    sizes = sizes.at[donor].add(-passed).at[receiver].add(passed)
    labels = jnp.searchsorted(jnp.cumsum(sizes), jnp.arange(rows * top), side="right").astype(jnp.int32)
    table = labels.reshape(top, rows).T
    table = table[jax.random.permutation(jax.random.fold_in(own, 1), rows)]
    offset_by = jax.random.randint(jax.random.fold_in(own, 2), (rows, 1), 0, top)
    return jnp.take_along_axis(table, (jnp.arange(top)[None, :] + offset_by) % top, axis=1)


def load_shares(amount, total, most, slope, full):
    weights = [(1 << 20) // math.isqrt(grade ** slope) + 1 for grade in range(1, amount + 1)]
    largest = most if full else min(most, max(-(-total // amount), total * weights[0] // sum(weights)))
    least = 1 if total - largest >= amount - 1 else 0
    counts, surplus = [largest] + [least] * (amount - 1), total - largest - least * (amount - 1)
    while surplus > 0:
        movable = [i for i in range(1, amount) if counts[i] < largest] or [i for i in range(1, amount) if counts[i] < most]
        pool, left = sum([weights[i] for i in movable]), surplus
        for i in movable:
            more = min(most - counts[i], max(1, left * weights[i] // pool), surplus)
            counts[i] = counts[i] + more
            surplus = surplus - more
    return np.array(counts)


def bell_draw(own_key, dims, scale, reach, cuts=(), held_as=jnp.bfloat16):
    drawn = scale * jax.random.normal(own_key, dims, jnp.float32)
    if cuts:
        drawn = drawn * level_of(own_key, dims, cuts, -0.22, 0.18)
    return jnp.clip(drawn, -reach, reach).astype(held_as)


def setup_inputs(seed: int = 0) -> dict:
    keys = jax.random.split(jax.random.key(seed), 21)
    block_input = draw_block_input(jax.random.fold_in(keys[20], 71), 0)
    out_grad = bell_draw(keys[1], (TOKENS, D), 1.0, 6.0, ((0, 32),), jnp.float32)
    segments = jnp.searchsorted(jnp.cumsum(uneven_parts(keys[2], max(4, TOKENS // 800), TOKENS, min(2000, TOKENS // 2), 1)), jnp.arange(TOKENS), side="right").astype(jnp.int32)
    routes_keys = jax.random.split(jax.random.fold_in(keys[3], 1), TOKENS // ROWS)
    routes_turns = jax.random.permutation(jax.random.fold_in(keys[3], 3), TOKENS // ROWS)
    routes = jax.vmap(lambda own, number: routed_block(jax.random.fold_in(keys[3], 2), own, number, ROWS, EXPERTS, TOPK, CAP, 2))(routes_keys, routes_turns).reshape((TOKENS, TOPK))
    route_weight = jnp.clip(0.1 + 0.5 * jax.random.uniform(keys[4], (TOKENS, TOPK), jnp.float32) ** level_of(keys[4], (TOKENS, TOPK), ((0, 8),), -0.2, 0.2), 0.1, 0.6)
    norm_attn = jnp.clip(1.0 + 0.1 * jax.random.normal(keys[5], (D,), jnp.float32), 0.5, 1.5).astype(jnp.bfloat16)
    query_down = bell_draw(keys[6], (D, QRANK), D ** -0.5, 0.125, ((0, 32),))
    query_norm = jnp.clip(1.0 + 0.1 * jax.random.normal(keys[7], (QRANK,), jnp.float32), 0.5, 1.5).astype(jnp.bfloat16)
    query_up = bell_draw(keys[8], (QRANK, HEADS * (NOPE + ROPE)), QRANK ** -0.5, 0.15625, ((0, 8), (1, 4)))
    latent_down = bell_draw(keys[9], (D, KVRANK + ROPE), D ** -0.5, 0.125, ((0, 32),))
    latent_norm = jnp.clip(1.0 + 0.1 * jax.random.normal(keys[10], (KVRANK,), jnp.float32), 0.5, 1.5).astype(jnp.bfloat16)
    latent_up = bell_draw(keys[11], (KVRANK, HEADS * (NOPE + VDIM)), KVRANK ** -0.5, 0.25, ((0, 8), (1, 4)))
    out_proj = bell_draw(keys[12], (D, HEADS * VDIM), (HEADS * VDIM // 64) ** -0.5, 1.0, ((0, 8), (1, 4)))
    norm_ffn = jnp.clip(1.0 + 0.1 * jax.random.normal(keys[13], (D,), jnp.float32), 0.5, 1.5).astype(jnp.bfloat16)
    shared_gate = bell_draw(keys[14], (D, SHARED), D ** -0.5, 0.125, ((0, 8), (1, 4)))
    shared_up = bell_draw(keys[15], (D, SHARED), D ** -0.5, 0.125, ((0, 8), (1, 4)))
    shared_down = bell_draw(keys[16], (D, SHARED), SHARED ** -0.5, 0.109375, ((0, 8), (1, 4)))
    expert_gate = bell_draw(keys[17], (EXPERTS, D, FF), D ** -0.5, 0.125, ((0, 8), (2, 4)))
    expert_up = bell_draw(keys[18], (EXPERTS, D, FF), D ** -0.5, 0.125, ((0, 8), (2, 4)))
    expert_down = bell_draw(keys[19], (EXPERTS, D, FF), FF ** -0.5, 0.15625, ((0, 8), (2, 4)))
    return dict(block_input=block_input, out_grad=out_grad, segments=segments, routes=routes, route_weight=route_weight, norm_attn=norm_attn, query_down=query_down, query_norm=query_norm, query_up=query_up, latent_down=latent_down, latent_norm=latent_norm, latent_up=latent_up, out_proj=out_proj, norm_ffn=norm_ffn, shared_gate=shared_gate, shared_up=shared_up, shared_down=shared_down, expert_gate=expert_gate, expert_up=expert_up, expert_down=expert_down)


EPS = 1e-06
THETA = 50000.0

def as_single(values):
    return values.astype(jnp.float32)

def rounded(values):
    return lax.optimization_barrier(values.astype(jnp.bfloat16))

def round_trip(values):
    return as_single(rounded(values))

def product(left, right):
    return jnp.dot(left, right, preferred_element_type=jnp.float32)

def rms_scale(values):
    return lax.rsqrt(lax.optimization_barrier(jnp.mean(values * values, axis=-1, keepdims=True)) + EPS)

def norm_back(grad, normed, scale, gain):
    scaled = grad * gain
    return scale * (scaled - normed * lax.optimization_barrier(jnp.mean(scaled * normed, axis=-1, keepdims=True)))

def angles(count):
    half = ROPE // 2
    freq = THETA ** (-jnp.arange(half, dtype=jnp.float32) * 2.0 / ROPE)
    phase = as_single(jnp.arange(count, dtype=jnp.int32) % SEQ)[:, None] * freq[None, :]
    return (jnp.cos(phase), jnp.sin(phase))

def rotate(values, cosine, sine):
    half = values.shape[-1] // 2
    first = values[..., :half]
    second = values[..., half:]
    return jnp.concatenate([first * cosine - second * sine, second * cosine + first * sine], axis=-1)

def unrotate(values, cosine, sine):
    half = values.shape[-1] // 2
    first = values[..., :half]
    second = values[..., half:]
    return jnp.concatenate([first * cosine + second * sine, second * cosine - first * sine], axis=-1)

def scores_of(query_nope, query_rope, key_nope, rope_key, segment):
    scale = 1.0 / math.sqrt(NOPE + ROPE)
    scores = jnp.einsum('qhd,khd->hqk', as_single(query_nope), as_single(key_nope))
    scores = scores + jnp.einsum('qhd,kd->hqk', as_single(query_rope), as_single(rope_key))
    places = jnp.arange(SEQ, dtype=jnp.int32)
    mask = (places[:, None] >= places[None, :]) & (segment[:, None] == segment[None, :])
    return jnp.where(mask[None], scores * scale, -jnp.inf)

def attend(pieces):
    query_nope, query_rope, key_nope, rope_key, values, segment = pieces
    scores = scores_of(query_nope, query_rope, key_nope, rope_key, segment)
    total = jax.nn.logsumexp(scores, axis=-1)
    probs = round_trip(jnp.exp(scores - total[..., None]))
    mixed = rounded(jnp.einsum('hqk,khd->qhd', probs, as_single(values)))
    return (mixed, total)

def attend_back(pieces):
    query_nope, query_rope, key_nope, rope_key, values, segment, total, d_mixed = pieces
    scale = 1.0 / math.sqrt(NOPE + ROPE)
    scores = scores_of(query_nope, query_rope, key_nope, rope_key, segment)
    probs = jnp.exp(scores - total[..., None])
    probs_low = round_trip(probs)
    d_out = as_single(d_mixed)
    d_values = jnp.einsum('hqk,qhd->khd', probs_low, d_out)
    d_probs = jnp.einsum('qhd,khd->hqk', d_out, as_single(values))
    delta = lax.optimization_barrier(jnp.sum(probs * d_probs, axis=-1, keepdims=True))
    d_scores = round_trip(probs * (d_probs - delta) * scale)
    d_query_nope = jnp.einsum('hqk,khd->qhd', d_scores, as_single(key_nope))
    d_query_rope = jnp.einsum('hqk,kd->qhd', d_scores, as_single(rope_key))
    d_key_nope = jnp.einsum('hqk,qhd->khd', d_scores, as_single(query_nope))
    d_rope_key = jnp.einsum('hqk,qhd->kd', d_scores, as_single(query_rope))
    return (d_query_nope, d_query_rope, d_key_nope, d_rope_key, d_values)

def slot_table(route_rows, weight_rows, blocks, capacity, experts):
    count = route_rows.shape[0]
    flat_route = route_rows.reshape(blocks, -1)
    onehot = (flat_route[:, :, None] == jnp.arange(experts, dtype=jnp.int32)[None, None, :]).astype(jnp.int32)
    before = jnp.cumsum(onehot, axis=1) - onehot
    rank = lax.optimization_barrier(jnp.sum(before * onehot, axis=2))
    block_id = jnp.arange(blocks, dtype=jnp.int32)[:, None]
    slot = (flat_route * (blocks * capacity) + block_id * capacity + rank).reshape(-1).astype(jnp.int32)
    token = jnp.repeat(jnp.arange(count, dtype=jnp.int32), route_rows.shape[1])
    total = experts * blocks * capacity
    source = jnp.full((total,), count, jnp.int32).at[slot].set(token)
    weight = jnp.zeros((total,), jnp.float32).at[slot].set(as_single(weight_rows).reshape(-1))
    return (slot, source, weight)

def reference(block_input, out_grad, segments, routes, route_weight, norm_attn, query_down, query_norm, query_up, latent_down, latent_norm, latent_up, out_proj, norm_ffn, shared_gate, shared_up, shared_down, expert_gate, expert_up, expert_down):
    gain_attn = as_single(norm_attn)
    gain_query = as_single(query_norm)
    gain_key = as_single(latent_norm)
    gain_ffn = as_single(norm_ffn)
    sequences = TOKENS // SEQ
    scale_in = rms_scale(block_input)
    normed_in = block_input * scale_in
    hidden_in = rounded(normed_in * gain_attn)
    query_raw = product(hidden_in, query_down)
    scale_query = rms_scale(query_raw)
    normed_query = query_raw * scale_query
    query_latent = rounded(normed_query * gain_query)
    latent_raw = product(hidden_in, latent_down)
    key_raw = latent_raw[:, :KVRANK]
    scale_key = rms_scale(key_raw)
    normed_key = key_raw * scale_key
    key_latent = rounded(normed_key * gain_key)
    cosine, sine = angles(TOKENS)
    rope_key = rounded(rotate(latent_raw[:, KVRANK:], cosine, sine))
    query_full = product(query_latent, query_up).reshape(TOKENS, HEADS, NOPE + ROPE)
    query_nope = rounded(query_full[..., :NOPE])
    query_rope = rounded(rotate(query_full[..., NOPE:], cosine[:, None, :], sine[:, None, :]))
    key_value = rounded(product(key_latent, latent_up)).reshape(TOKENS, HEADS, NOPE + VDIM)
    key_nope = key_value[..., :NOPE]
    values = key_value[..., NOPE:]
    pieces = (query_nope.reshape(sequences, SEQ, HEADS, NOPE), query_rope.reshape(sequences, SEQ, HEADS, ROPE), key_nope.reshape(sequences, SEQ, HEADS, NOPE), rope_key.reshape(sequences, SEQ, ROPE), values.reshape(sequences, SEQ, HEADS, VDIM), segments.reshape(sequences, SEQ))
    mixed, totals = lax.map(attend, pieces)
    attended = mixed.reshape(TOKENS, HEADS * VDIM)
    mid = block_input + product(attended, out_proj.T)
    scale_mid = rms_scale(mid)
    normed_mid = mid * scale_mid
    hidden_mid = rounded(normed_mid * gain_ffn)
    shared_gate_val = product(hidden_mid, shared_gate)
    shared_up_val = product(hidden_mid, shared_up)
    shared_act = rounded(jax.nn.silu(shared_gate_val) * shared_up_val)
    shared_out = product(shared_act, shared_down.T)
    grad_low = rounded(out_grad)
    blocks = TOKENS // ROWS
    slot_ids, source, slot_weight = slot_table(routes, route_weight, blocks, CAP, EXPERTS)
    per_expert = blocks * CAP
    source = source.reshape(EXPERTS, per_expert)
    slot_weight = slot_weight.reshape(EXPERTS, per_expert)
    hidden_pad = jnp.concatenate([hidden_mid, jnp.zeros((1, D), jnp.bfloat16)], axis=0)
    grad_pad = jnp.concatenate([grad_low, jnp.zeros((1, D), jnp.bfloat16)], axis=0)
    width = FF // N_TENSOR

    def expert_step(carry, items):
        routed, back = carry
        rows, weight, gate_w, up_w, down_w = items
        inputs = hidden_pad[rows]
        gate_val = product(inputs, gate_w)
        up_val = product(inputs, up_w)
        act = rounded(jax.nn.silu(gate_val) * up_val)
        output = jnp.zeros((rows.shape[0], D), jnp.float32)
        for block in range(N_TENSOR):
            part = slice(block * width, (block + 1) * width)
            output = output + round_trip(product(act[:, part], down_w[:, part].T))
        grads_in = rounded(weight[:, None] * as_single(grad_pad[rows]))
        d_act = product(grads_in, down_w)
        g_down = product(grads_in.T, act)
        sigma = jax.nn.sigmoid(gate_val)
        d_gate = rounded(d_act * up_val * sigma * (1.0 + gate_val * (1.0 - sigma)))
        d_up = rounded(d_act * gate_val * sigma)
        g_gate = product(inputs.T, d_gate)
        g_up = product(inputs.T, d_up)
        back_rows = jnp.zeros((rows.shape[0], D), jnp.float32)
        for block in range(N_TENSOR):
            part = slice(block * width, (block + 1) * width)
            back_rows = back_rows + round_trip(product(d_gate[:, part], gate_w[:, part].T) + product(d_up[:, part], up_w[:, part].T))
        routed = routed.at[rows].add(weight[:, None] * output)
        back = back.at[rows].add(back_rows)
        return ((routed, back), (g_gate, g_up, g_down))
    start = (jnp.zeros((TOKENS + 1, D), jnp.float32), jnp.zeros((TOKENS + 1, D), jnp.float32))
    (routed, routed_back), expert_grads = lax.scan(expert_step, start, (source, slot_weight, expert_gate, expert_up, expert_down))
    grad_expert_gate, grad_expert_up, grad_expert_down = expert_grads
    block_output = mid + shared_out + routed[:TOKENS]
    d_shared_act = product(grad_low, shared_down)
    grad_shared_down = product(grad_low.T, shared_act)
    sigma = jax.nn.sigmoid(shared_gate_val)
    d_shared_gate = rounded(d_shared_act * shared_up_val * sigma * (1.0 + shared_gate_val * (1.0 - sigma)))
    d_shared_up = rounded(d_shared_act * shared_gate_val * sigma)
    grad_shared_gate = product(hidden_mid.T, d_shared_gate)
    grad_shared_up = product(hidden_mid.T, d_shared_up)
    d_hidden_mid = product(d_shared_gate, shared_gate.T) + product(d_shared_up, shared_up.T) + routed_back[:TOKENS]
    grad_norm_ffn = lax.optimization_barrier(jnp.sum(d_hidden_mid * normed_mid, axis=0))
    d_mid = out_grad + norm_back(d_hidden_mid, normed_mid, scale_mid, gain_ffn)
    mid_low = rounded(d_mid)
    grad_out_proj = product(mid_low.T, attended)
    d_attended = rounded(product(mid_low, out_proj)).reshape(sequences, SEQ, HEADS, VDIM)
    back_pieces = pieces + (totals, d_attended)
    d_query_nope, d_query_rope, d_key_nope, d_rope_key, d_values = lax.map(attend_back, back_pieces)
    d_query_nope = d_query_nope.reshape(TOKENS, HEADS, NOPE)
    d_query_rope = unrotate(d_query_rope.reshape(TOKENS, HEADS, ROPE), cosine[:, None, :], sine[:, None, :])
    d_query = rounded(jnp.concatenate([d_query_nope, d_query_rope], axis=-1)).reshape(TOKENS, HEADS * (NOPE + ROPE))
    grad_query_up = product(query_latent.T, d_query)
    d_query_latent = product(d_query, query_up.T)
    d_key_value = rounded(jnp.concatenate([d_key_nope.reshape(TOKENS, HEADS, NOPE), d_values.reshape(TOKENS, HEADS, VDIM)], axis=-1)).reshape(TOKENS, HEADS * (NOPE + VDIM))
    grad_latent_up = product(key_latent.T, d_key_value)
    d_key_latent = product(d_key_value, latent_up.T)
    grad_query_norm = lax.optimization_barrier(jnp.sum(d_query_latent * normed_query, axis=0))
    d_query_raw = rounded(norm_back(d_query_latent, normed_query, scale_query, gain_query))
    grad_latent_norm = lax.optimization_barrier(jnp.sum(d_key_latent * normed_key, axis=0))
    d_key_raw = norm_back(d_key_latent, normed_key, scale_key, gain_key)
    d_rope_raw = unrotate(d_rope_key.reshape(TOKENS, ROPE), cosine, sine)
    d_latent_raw = rounded(jnp.concatenate([d_key_raw, d_rope_raw], axis=-1))
    grad_query_down = product(hidden_in.T, d_query_raw)
    grad_latent_down = product(hidden_in.T, d_latent_raw)
    d_hidden_in = product(d_query_raw, query_down.T) + product(d_latent_raw, latent_down.T)
    grad_norm_attn = lax.optimization_barrier(jnp.sum(d_hidden_in * normed_in, axis=0))
    input_grad = d_mid + norm_back(d_hidden_in, normed_in, scale_in, gain_attn)
    return (block_output, input_grad, grad_norm_attn, grad_query_down, grad_query_norm, grad_query_up, grad_latent_down, grad_latent_norm, grad_latent_up, grad_out_proj, grad_norm_ffn, grad_shared_gate, grad_shared_up, grad_shared_down, grad_expert_gate, grad_expert_up, grad_expert_down)
```

```python
import math

import jax
import jax.numpy as jnp
from jax import lax
from jax.sharding import PartitionSpec as P

NOPE = 128
ROPE = 64
VDIM = 128
KVRANK = 512
SEQ = 512


EPS = 1e-06
THETA = 50000.0


def as_half(values):
    return values.astype(jnp.bfloat16)


def as_single(values):
    return values.astype(jnp.float32)


def product(left, right):
    return jnp.dot(left, right, preferred_element_type=jnp.float32)


def contract_rows(left, right):
    return lax.dot_general(
        left, right, (((0,), (0,)), ((), ())), preferred_element_type=jnp.float32
    )


def against_rows(left, right):
    return lax.dot_general(
        left, right, (((1,), (1,)), ((), ())), preferred_element_type=jnp.float32
    )


def rms_scale(values):
    return lax.rsqrt(jnp.mean(values * values, axis=-1, keepdims=True) + EPS)


def norm_back(grad, normed, scale, gain):
    scaled = grad * gain
    return scale * (scaled - normed * jnp.mean(scaled * normed, axis=-1, keepdims=True))


def angles(positions):
    half = ROPE // 2
    freq = THETA ** (-jnp.arange(half, dtype=jnp.float32) * 2.0 / ROPE)
    phase = as_single(positions)[:, None] * freq[None, :]
    return (jnp.cos(phase), jnp.sin(phase))


def rotate(values, cosine, sine):
    half = values.shape[-1] // 2
    first = values[..., :half]
    second = values[..., half:]
    return jnp.concatenate(
        [first * cosine - second * sine, second * cosine + first * sine], axis=-1
    )


def unrotate(values, cosine, sine):
    half = values.shape[-1] // 2
    first = values[..., :half]
    second = values[..., half:]
    return jnp.concatenate(
        [first * cosine + second * sine, second * cosine - first * sine], axis=-1
    )


def score_block(query_nope, query_rope, key_nope, rope_key, mask):
    scale = 1.0 / math.sqrt(NOPE + ROPE)
    scores = jnp.einsum("qhd,khd->hqk", query_nope, key_nope, preferred_element_type=jnp.float32)
    scores = scores + jnp.einsum(
        "qhd,kd->hqk", query_rope, rope_key, preferred_element_type=jnp.float32
    )
    return jnp.where(mask[None], scores * scale, -jnp.inf)


LANES = 128


def padded_width(width):
    return -(-width // LANES) * LANES


def swap(rows, mask):
    count = lax.axis_size("dp")
    return lax.ppermute(rows, "dp", [(i, i ^ mask) for i in range(count)])


def four_chips():
    return lax.axis_size("dp") == 2 * 2 * 2


def fetch_chunks(rows):
    half = rows.shape[0] // 2
    along = swap(rows, 2)
    across = swap(rows, 4)
    side = swap(rows, 1)
    first = swap(along[:half], 4)
    second = swap(across[half:], 2)
    corner = jnp.concatenate([first, second], axis=0)
    return {
        0: rows,
        1: side,
        2: along,
        3: swap(along, 1),
        4: across,
        5: swap(across, 1),
        6: corner,
        7: swap(corner, 1),
    }


def spread(rows):
    if four_chips():
        chunks = fetch_chunks(rows)
        return [jnp.concatenate([chunks[m], chunks[m | 1]], axis=0) for m in (0, 2, 4, 6)]
    rounds = max(1, lax.axis_size("dp") // 8)
    size = rows.shape[0] // rounds
    return [rows[i * size : (i + 1) * size] for i in range(rounds)]


def ready(blocks, before):
    if four_chips():
        return blocks
    if before is not None:
        blocks, _ = lax.optimization_barrier((blocks, before))
    return tuple(lax.all_gather(block, "dp", axis=0, tiled=True) for block in blocks)


def hand_over(block):
    if four_chips():
        return block
    return lax.psum_scatter(block, "dp", scatter_dimension=0, tiled=True)


def collect(blocks):
    if four_chips():
        total = None
        for mask, block in zip((0, 2, 4, 6), blocks):
            count = block.shape[0] // 2
            other = swap(block[count:], 1)
            part = as_single(block[:count]) + as_single(other)
            if mask:
                part = as_single(swap(as_half(part), mask))
            total = part if total is None else total + part
        return total
    return as_single(jnp.concatenate(blocks, axis=0))


def gather_ordered(rows):
    if not four_chips():
        return lax.all_gather(rows, "dp", axis=0, tiled=True)
    place = lax.axis_index("dp")
    count = rows.shape[0]
    whole = jnp.zeros((count * lax.axis_size("dp"), rows.shape[1]), rows.dtype)
    for mask, chunk in fetch_chunks(rows).items():
        whole = lax.dynamic_update_slice(whole, chunk, ((place ^ mask) * count, 0))
    return whole


def scatter_ordered(rows):
    if not four_chips():
        return lax.psum_scatter(rows, "dp", scatter_dimension=0, tiled=True)
    place = lax.axis_index("dp")
    count = rows.shape[0] // lax.axis_size("dp")

    def part(mask):
        return lax.dynamic_slice_in_dim(rows, (place ^ mask) * count, count, axis=0)

    blocks = [jnp.concatenate([part(m), part(m | 1)], axis=0) for m in (0, 2, 4, 6)]
    return as_half(collect(blocks))


def gather_rows(rows):
    return lax.all_gather(rows, "tensor", axis=0, tiled=True)


def scatter_rows(rows):
    return as_single(
        lax.psum_scatter(as_half(rows), "tensor", scatter_dimension=0, tiled=True)
    )


def exchange(block):
    return lax.all_to_all(block, "dp", split_axis=0, concat_axis=0, tiled=True)


def split_units(weights):
    dp_count = lax.axis_size("dp")
    rows, units = weights[0].shape
    share = units // dp_count
    stacked = jnp.stack(weights).reshape(3, rows, dp_count, share).transpose(2, 0, 1, 3)
    got = exchange(stacked.reshape(dp_count, 3 * rows, share)).reshape(dp_count, 3, rows, share)
    return got.transpose(1, 0, 2, 3).reshape(3, dp_count * rows, share)


def join_units(grads):
    dp_count = lax.axis_size("dp")
    all_rows, share = grads[0].shape
    rows = all_rows // dp_count
    stacked = jnp.stack(grads).reshape(3, dp_count, rows, share).transpose(1, 0, 2, 3)
    got = exchange(stacked.reshape(dp_count, 3 * rows, share)).reshape(dp_count, 3, rows, share)
    return got.transpose(1, 2, 0, 3).reshape(3, rows, dp_count * share)


def pad_columns(values, width):
    return jnp.pad(values, ((0, 0), (0, width - values.shape[1])))


def join_columns(experts_weight, shared_slice):
    wide = padded_width(experts_weight.shape[2])
    parts = [pad_columns(experts_weight[e], wide) for e in range(experts_weight.shape[0])]
    parts.append(pad_columns(shared_slice, padded_width(shared_slice.shape[1])))
    return jnp.concatenate(parts, axis=1)


def body(
    block_input,
    out_grad,
    segments,
    routes,
    route_weight,
    norm_attn,
    query_down,
    query_norm,
    query_up,
    latent_down,
    latent_norm,
    latent_up,
    out_proj,
    norm_ffn,
    shared_gate,
    shared_up,
    shared_down,
    expert_gate,
    expert_up,
    expert_down,
):
    dp_count = lax.axis_size("dp")
    place = lax.axis_index("dp")
    quarter = lax.axis_index("tensor")
    own_rows = block_input.shape[0]
    group_rows = segments.shape[0]
    local_experts, model, expert_units = expert_gate.shape
    experts = local_experts * dp_count
    q_rank = query_down.shape[1]
    raw_width = q_rank + latent_down.shape[1]
    shard = query_down.shape[0]
    q_shard = query_norm.shape[0]

    packed_own = jnp.concatenate(
        [
            query_down,
            latent_down,
            norm_attn[:, None],
            norm_ffn[:, None],
            jnp.concatenate([query_norm, latent_norm])[:, None],
        ],
        axis=1,
    )
    packed = gather_ordered(gather_rows(packed_own))
    up_q = gather_ordered(query_up)
    up_kv = gather_ordered(latent_up)
    proj_out = lax.all_gather(out_proj, "dp", axis=0, tiled=True)
    gains = as_single(packed[:, raw_width:]).T
    gain_attn = gains[0]
    gain_ffn = gains[1]
    rank_gains = gains[2].reshape(-1, shard)
    gain_query = rank_gains[:, :q_shard].reshape(-1)
    gain_key = rank_gains[:, q_shard:].reshape(-1)

    chosen = routes[:, :, None] == jnp.arange(experts, dtype=jnp.int32)[None, None, :]
    dense_weight = jnp.sum(jnp.where(chosen, route_weight[:, :, None], 0.0), axis=1)
    weight_blocks = spread(dense_weight)
    grad_blocks = spread(gather_rows(as_half(out_grad)))

    sg, su, sd = split_units([shared_gate, shared_up, shared_down])
    cat_gate = join_columns(expert_gate, sg)
    cat_up = join_columns(expert_up, su)
    cat_down = join_columns(expert_down, sd)
    wide = padded_width(expert_units)
    column = jnp.arange(cat_gate.shape[1], dtype=jnp.int32)[None, :]

    scale_in = rms_scale(block_input)
    normed_in = block_input * scale_in
    hidden_in = as_half(normed_in * gain_attn)
    raw = product(hidden_in, packed)
    query_raw = raw[:, :q_rank]
    scale_query = rms_scale(query_raw)
    normed_query = query_raw * scale_query
    query_latent = as_half(normed_query * gain_query)
    key_raw = raw[:, q_rank : q_rank + KVRANK]
    scale_key = rms_scale(key_raw)
    normed_key = key_raw * scale_key
    key_latent = as_half(normed_key * gain_key)
    own_positions = (quarter * own_rows + jnp.arange(own_rows, dtype=jnp.int32)) % SEQ
    cos_own, sin_own = angles(own_positions)
    rope_own = as_half(rotate(raw[:, q_rank + KVRANK : raw_width], cos_own, sin_own))
    latents = gather_rows(jnp.concatenate([query_latent, key_latent, rope_own], axis=1))
    query_all = latents[:, :q_rank]
    key_all = latents[:, q_rank : q_rank + KVRANK]
    rope_all = latents[:, q_rank + KVRANK :]
    heads = up_q.shape[1] // (NOPE + ROPE)
    cos_all, sin_all = angles(jnp.arange(group_rows, dtype=jnp.int32) % SEQ)
    query_full = product(query_all, up_q).reshape(group_rows, heads, NOPE + ROPE)
    query_nope = as_half(query_full[..., :NOPE])
    query_rope = as_half(rotate(query_full[..., NOPE:], cos_all[:, None, :], sin_all[:, None, :]))
    key_value = as_half(product(key_all, up_kv)).reshape(group_rows, heads, NOPE + VDIM)
    key_nope = key_value[..., :NOPE]
    values = key_value[..., NOPE:]
    places = jnp.arange(SEQ, dtype=jnp.int32)
    causal = places[:, None] >= places[None, :]
    mask = causal & (segments[:, None] == segments[None, :])
    scores = score_block(query_nope, query_rope, key_nope, rope_all, mask)
    total = jax.nn.logsumexp(scores, axis=-1)
    probs = as_half(jnp.exp(scores - total[..., None]))
    mixed = jnp.einsum("hqk,khd->qhd", probs, values, preferred_element_type=jnp.float32)
    attended = as_half(mixed).reshape(group_rows, heads * VDIM)
    mid = block_input + scatter_rows(against_rows(attended, proj_out))
    scale_mid = rms_scale(mid)
    normed_mid = mid * scale_mid
    hidden_mid = as_half(normed_mid * gain_ffn)

    hidden_blocks = spread(gather_rows(hidden_mid))
    back_blocks = []
    act_blocks = []
    grad_gate = grad_up = grad_down = None
    for blocks in zip(hidden_blocks, grad_blocks, weight_blocks):
        hidden, grad, weights = ready(blocks, (back_blocks[-1], more) if back_blocks else None)
        mine = lax.dynamic_slice_in_dim(weights, place * local_experts, local_experts, axis=1)
        factor = jnp.ones((1, 1), jnp.float32)
        for e in range(local_experts):
            inside = (column >= e * wide) & (column < (e + 1) * wide)
            factor = jnp.where(inside, mine[:, e : e + 1], factor)
        gate_val = product(hidden, cat_gate)
        up_val = product(hidden, cat_up)
        d_act = product(grad, cat_down) * factor
        sigma = jax.nn.sigmoid(gate_val)
        act = as_half(gate_val * sigma * up_val)
        act = as_half(as_single(act) * factor)
        d_gate = as_half(d_act * up_val * sigma * (1.0 + gate_val * (1.0 - sigma)))
        d_up = as_half(d_act * gate_val * sigma)
        back = as_half(against_rows(d_gate, cat_gate) + against_rows(d_up, cat_up))
        back_blocks.append(hand_over(back))
        act_blocks.append(act)
        more = (
            contract_rows(hidden, d_gate),
            contract_rows(hidden, d_up),
            contract_rows(grad, act),
        )
        if grad_gate is None:
            grad_gate, grad_up, grad_down = more
        else:
            grad_gate, grad_up, grad_down = (
                grad_gate + more[0],
                grad_up + more[1],
                grad_down + more[2],
            )
    d_hidden_mid = scatter_rows(collect(back_blocks))

    def cut(grads):
        return jnp.stack(
            [grads[:, e * wide : e * wide + expert_units] for e in range(local_experts)]
        )

    share = sg.shape[1]
    grad_gate_sh, grad_up_sh, grad_down_sh = as_single(
        join_units(
            [
                as_half(g[:, local_experts * wide : local_experts * wide + share])
                for g in (grad_gate, grad_up, grad_down)
            ]
        )
    )

    grad_gain_ffn = jnp.sum(d_hidden_mid * normed_mid, axis=0)
    d_mid = out_grad + norm_back(d_hidden_mid, normed_mid, scale_mid, gain_ffn)
    mid_low = as_half(d_mid)
    act_blocks, mid_low = lax.optimization_barrier((act_blocks, mid_low))
    out_blocks = []
    for act in act_blocks:
        if out_blocks and not four_chips():
            act, _ = lax.optimization_barrier((act, out_blocks[-1]))
        out_blocks.append(hand_over(as_half(against_rows(act, cat_down))))
    block_output = mid + scatter_rows(collect(out_blocks))

    mid_all = gather_rows(mid_low)
    grad_proj_out = contract_rows(mid_all, attended)
    d_attended = as_half(product(mid_all, proj_out)).reshape(group_rows, heads, VDIM)
    scale = 1.0 / math.sqrt(NOPE + ROPE)
    scores = score_block(query_nope, query_rope, key_nope, rope_all, mask)
    probs = jnp.exp(scores - total[..., None])
    probs_low = as_half(probs)
    value_grads = jnp.einsum(
        "hqk,qhd->khd", probs_low, d_attended, preferred_element_type=jnp.float32
    )
    d_probs = jnp.einsum("qhd,khd->hqk", d_attended, values, preferred_element_type=jnp.float32)
    delta = jnp.sum(probs * d_probs, axis=-1, keepdims=True)
    d_scores = as_half(probs * (d_probs - delta) * scale)
    query_nope_grads = jnp.einsum(
        "hqk,khd->qhd", d_scores, key_nope, preferred_element_type=jnp.float32
    )
    query_rope_grads = jnp.einsum(
        "hqk,kd->qhd", d_scores, rope_all, preferred_element_type=jnp.float32
    )
    key_nope_grads = jnp.einsum(
        "hqk,qhd->khd", d_scores, query_nope, preferred_element_type=jnp.float32
    )
    rope_key_grads = jnp.einsum(
        "hqk,qhd->kd", d_scores, query_rope, preferred_element_type=jnp.float32
    )
    d_query_rope = unrotate(query_rope_grads, cos_all[:, None, :], sin_all[:, None, :])
    d_query = as_half(jnp.concatenate([query_nope_grads, d_query_rope], axis=-1)).reshape(
        group_rows, heads * (NOPE + ROPE)
    )
    grad_up_q = contract_rows(query_all, d_query)
    d_query_latent = against_rows(d_query, up_q)
    d_key_value = as_half(jnp.concatenate([key_nope_grads, value_grads], axis=-1)).reshape(
        group_rows, heads * (NOPE + VDIM)
    )
    grad_up_kv = contract_rows(key_all, d_key_value)
    d_key_latent = against_rows(d_key_value, up_kv)
    d_latents = scatter_rows(
        jnp.concatenate(
            [as_half(d_query_latent), as_half(d_key_latent), as_half(rope_key_grads)], axis=1
        )
    )
    latent_q = d_latents[:, :q_rank]
    latent_k = d_latents[:, q_rank : q_rank + KVRANK]
    latent_r = d_latents[:, q_rank + KVRANK :]
    grad_gain_query = jnp.sum(latent_q * normed_query, axis=0)
    d_query_raw = norm_back(latent_q, normed_query, scale_query, gain_query)
    grad_gain_key = jnp.sum(latent_k * normed_key, axis=0)
    d_key_raw = norm_back(latent_k, normed_key, scale_key, gain_key)
    d_rope_raw = unrotate(latent_r, cos_own, sin_own)
    extra = packed.shape[1] - raw_width
    d_raw = as_half(
        jnp.concatenate(
            [d_query_raw, d_key_raw, d_rope_raw, jnp.zeros((own_rows, extra), jnp.float32)], axis=1
        )
    )
    d_hidden_in = against_rows(d_raw, packed)
    grad_gain_attn = jnp.sum(d_hidden_in * normed_in, axis=0)
    input_grad = d_mid + norm_back(d_hidden_in, normed_in, scale_in, gain_attn)
    rank_grads = jnp.concatenate(
        [grad_gain_query.reshape(-1, q_shard), grad_gain_key.reshape(-1, shard - q_shard)], axis=1
    ).reshape(-1)
    gain_grads = jnp.stack([grad_gain_attn, grad_gain_ffn, rank_grads], axis=1)
    packed_grads = contract_rows(hidden_in, d_raw) + jnp.pad(gain_grads, ((0, 0), (raw_width, 0)))
    down_out = scatter_rows(scatter_ordered(as_half(packed_grads)))
    gains_out = down_out[:, raw_width:]

    def scatter_dense(grads):
        return as_single(
            lax.psum_scatter(as_half(grads), "dp", scatter_dimension=0, tiled=True)
        )

    return (
        block_output,
        input_grad,
        gains_out[:, 0],
        down_out[:, :q_rank],
        gains_out[:q_shard, 2],
        scatter_dense(grad_up_q),
        down_out[:, q_rank:raw_width],
        gains_out[q_shard:, 2],
        scatter_dense(grad_up_kv),
        scatter_dense(grad_proj_out),
        gains_out[:, 1],
        grad_gate_sh,
        grad_up_sh,
        grad_down_sh,
        cut(grad_gate),
        cut(grad_up),
        cut(grad_down),
    )


def solution(mesh):
    in_specs = (
        P(("dp", "tensor"), None),
        P(("dp", "tensor"), None),
        P("dp"),
        P("dp", None),
        P("dp", None),
        P(("dp", "tensor")),
        P(("dp", "tensor"), None),
        P(("dp", "tensor")),
        P("dp", "tensor"),
        P(("dp", "tensor"), None),
        P(("dp", "tensor")),
        P("dp", "tensor"),
        P("dp", "tensor"),
        P(("dp", "tensor")),
        P("dp", "tensor"),
        P("dp", "tensor"),
        P("dp", "tensor"),
        P("dp", None, "tensor"),
        P("dp", None, "tensor"),
        P("dp", None, "tensor"),
    )
    out_specs = (
        P(("dp", "tensor"), None),
        P(("dp", "tensor"), None),
        P(("dp", "tensor")),
        P(("dp", "tensor"), None),
        P(("dp", "tensor")),
        P("dp", "tensor"),
        P(("dp", "tensor"), None),
        P(("dp", "tensor")),
        P("dp", "tensor"),
        P("dp", "tensor"),
        P(("dp", "tensor")),
        P("dp", "tensor"),
        P("dp", "tensor"),
        P("dp", "tensor"),
        P("dp", None, "tensor"),
        P("dp", None, "tensor"),
        P("dp", None, "tensor"),
    )
    return jax.shard_map(body, mesh=mesh, in_specs=in_specs, out_specs=out_specs, check_vma=False)
```

```python
import math

import jax
import jax.numpy as jnp
from jax import lax
from jax.experimental.layout import Layout, with_layout_constraint
from jax.sharding import PartitionSpec as P

NOPE = 128
ROPE = 64
VDIM = 128
KVRANK = 512
SEQ = 512


EPS = 1e-06
THETA = 50000.0


def as_half(values):
    return values.astype(jnp.bfloat16)


def as_single(values):
    return values.astype(jnp.float32)


def product(left, right):
    return jnp.dot(left, right, preferred_element_type=jnp.float32)


def contract_rows(left, right):
    return lax.dot_general(
        left, right, (((0,), (0,)), ((), ())), preferred_element_type=jnp.float32
    )


def against_rows(left, right):
    return lax.dot_general(
        left, right, (((1,), (1,)), ((), ())), preferred_element_type=jnp.float32
    )


def rms_scale(values):
    return lax.rsqrt(jnp.mean(values * values, axis=-1, keepdims=True) + EPS)


def norm_back(grad, normed, scale, gain):
    scaled = grad * gain
    return scale * (scaled - normed * jnp.mean(scaled * normed, axis=-1, keepdims=True))


def angles(positions):
    half = ROPE // 2
    freq = THETA ** (-jnp.arange(half, dtype=jnp.float32) * 2.0 / ROPE)
    phase = as_single(positions)[:, None] * freq[None, :]
    return (jnp.cos(phase), jnp.sin(phase))


def rotate(values, cosine, sine):
    half = values.shape[-1] // 2
    first = values[..., :half]
    second = values[..., half:]
    return jnp.concatenate(
        [first * cosine - second * sine, second * cosine + first * sine], axis=-1
    )


def unrotate(values, cosine, sine):
    half = values.shape[-1] // 2
    first = values[..., :half]
    second = values[..., half:]
    return jnp.concatenate(
        [first * cosine + second * sine, second * cosine - first * sine], axis=-1
    )


def score_block(query_nope, query_rope, key_nope, rope_key, mask):
    scale = 1.0 / math.sqrt(NOPE + ROPE)
    scores = jnp.einsum("qhd,khd->hqk", query_nope, key_nope, preferred_element_type=jnp.float32)
    scores = scores + jnp.einsum(
        "qhd,kd->hqk", query_rope, rope_key, preferred_element_type=jnp.float32
    )
    return jnp.where(mask[None], scores * scale, -jnp.inf)


def after(value, *before):
    return lax.optimization_barrier((value, before))[0]


def fold_rows(rows, base):
    _, width = rows.shape
    return rows.reshape(-1, base, width).transpose(1, 0, 2).reshape(base, -1)


def unfold_rows(rows, times):
    base = rows.shape[0]
    return rows.reshape(base, times, -1).transpose(1, 0, 2).reshape(base * times, -1)


def swap(rows, mask):
    count = lax.axis_size("dp")
    return lax.ppermute(rows, "dp", [(i, i ^ mask) for i in range(count)])


def four_chips():
    return lax.axis_size("dp") == 2 * 2 * 2


def fetch_chunks(rows):
    half = rows.shape[0] // 2
    along = swap(rows, 2)
    across = swap(rows, 4)
    side = swap(rows, 1)
    first = swap(along[:half], 4)
    second = swap(across[half:], 2)
    corner = jnp.concatenate([first, second], axis=0)
    return {
        0: rows,
        1: side,
        2: along,
        3: swap(along, 1),
        4: across,
        5: swap(across, 1),
        6: corner,
        7: swap(corner, 1),
    }


CHIPS = (0, 2, 4, 6)


def both_cores(rows):
    return jnp.concatenate([rows, swap(rows, 1)], axis=0)


def pair_sum(block):
    count = block.shape[0] // 2
    return as_half(as_single(block[:count]) + as_single(swap(block[count:], 1)))


def send_part(part, mask):
    return swap(part, mask) if mask else part


def add_parts(parts):
    total = as_single(parts[0])
    for part in parts[1:]:
        total = total + as_single(part)
    return as_half(total)


def scatter_plane(block):
    return lax.psum_scatter(block, "dp", scatter_dimension=0, tiled=True)


def gather_plane(block):
    return lax.all_gather(block, "dp", axis=0, tiled=True)


def gather_ordered(rows):
    if not four_chips():
        return lax.all_gather(rows, "dp", axis=0, tiled=True)
    place = lax.axis_index("dp")
    count = rows.shape[0]
    whole = jnp.zeros((count * lax.axis_size("dp"), rows.shape[1]), rows.dtype)
    for mask, chunk in fetch_chunks(rows).items():
        whole = lax.dynamic_update_slice(whole, chunk, ((place ^ mask) * count, 0))
    return with_layout_constraint(whole, Layout(major_to_minor=(0, 1)))


def reorder(values, axis):
    if not four_chips():
        return values
    place = lax.axis_index("dp")
    count = lax.axis_size("dp")
    size = values.shape[axis] // count
    return jnp.concatenate(
        [
            lax.dynamic_slice_in_dim(values, (place ^ m) * size, size, axis=axis)
            for m in range(count)
        ],
        axis=axis,
    )


def gather_reordered(rows):
    if not four_chips():
        return gather_plane(rows)
    chunks = fetch_chunks(rows)
    return jnp.concatenate([chunks[m] for m in range(len(chunks))], axis=0)


def parts_of(rows):
    count = rows.shape[0] // lax.axis_size("dp")

    def part(mask):
        return rows[mask * count : (mask + 1) * count]

    return [
        as_half(as_single(part(m)) + as_single(swap(part(m | 1), 1))) for m in CHIPS
    ]


def gather_rows(rows):
    return lax.all_gather(rows, "tensor", axis=0, tiled=True)


def scatter_rows(rows):
    return as_single(
        lax.psum_scatter(as_half(rows), "tensor", scatter_dimension=0, tiled=True)
    )


def exchange(block):
    return lax.all_to_all(block, "dp", split_axis=0, concat_axis=0, tiled=True)


def split_units(weights):
    dp_count = lax.axis_size("dp")
    rows, units = weights[0].shape
    share = units // dp_count
    stacked = jnp.stack([w.T for w in weights]).reshape(3, dp_count, share, rows)
    stacked = stacked.transpose(1, 0, 2, 3).reshape(dp_count, 3 * share, rows)
    got = exchange(stacked).reshape(dp_count, 3, share, rows)
    return got.transpose(1, 2, 0, 3).reshape(3, share, dp_count * rows)


def join_units(grads):
    dp_count = lax.axis_size("dp")
    share, all_rows = grads[0].shape
    rows = all_rows // dp_count
    stacked = jnp.stack(grads).reshape(3, share, dp_count, rows).transpose(2, 0, 1, 3)
    got = exchange(stacked.reshape(dp_count, 3 * share, rows)).reshape(dp_count, 3, share, rows)
    return [g.T for g in got.transpose(1, 0, 2, 3).reshape(3, dp_count * share, rows)]


def join_rows(experts_weight, shared_slice):
    count, model, units = experts_weight.shape
    return jnp.concatenate(
        [experts_weight.swapaxes(1, 2).reshape(count * units, model), shared_slice], axis=0
    )


def layer(
    block_input,
    out_grad,
    segments,
    routes,
    route_weight,
    norm_attn,
    query_down,
    query_norm,
    query_up,
    latent_down,
    latent_norm,
    latent_up,
    out_proj,
    norm_ffn,
    shared_gate,
    shared_up,
    shared_down,
    expert_gate,
    expert_up,
    expert_down,
):
    dp_count = lax.axis_size("dp")
    place = lax.axis_index("dp")
    quarter = lax.axis_index("tensor")
    own_rows = block_input.shape[0]
    group_rows = segments.shape[0]
    local_experts, model, expert_units = expert_gate.shape
    experts = local_experts * dp_count
    q_rank = query_down.shape[1]
    raw_width = q_rank + latent_down.shape[1]
    shard = query_down.shape[0]
    q_shard = query_norm.shape[0]

    packed_own = jnp.concatenate(
        [
            query_down,
            latent_down,
            norm_attn[:, None],
            norm_ffn[:, None],
            jnp.concatenate([query_norm, latent_norm])[:, None],
        ],
        axis=1,
    )
    packed_line = gather_rows(packed_own)
    base = latent_up.shape[0]
    denses = (query_up, latent_up, out_proj)
    times = [w.shape[0] // base for w in denses]
    ends = [0]
    for w in denses:
        ends.append(ends[-1] + w.size // base)
    chosen = routes[:, :, None] == jnp.arange(experts, dtype=jnp.int32)[None, None, :]
    dense_weight = jnp.sum(jnp.where(chosen, route_weight[:, :, None], 0.0), axis=1)
    upper = as_half(dense_weight)
    terms = jnp.concatenate([upper, as_half(dense_weight - as_single(upper))], axis=1)
    folds = [fold_rows(w, base) for w in (*denses, terms)]
    folded = gather_ordered(jnp.concatenate(after(folds, packed_own), axis=1))

    def unfold_whole(index):
        part = folded[:, ends[index] : ends[index + 1]]
        width = denses[index].shape[1]
        part = part.reshape(dp_count, base, times[index], width).transpose(0, 2, 1, 3)
        return part.reshape(-1, width)

    packed_line, folded = lax.optimization_barrier((packed_line, folded))
    up_q, up_kv, proj_out = (unfold_whole(i) for i in range(3))
    terms_all = folded[:, ends[3] :].reshape(dp_count, base, group_rows // base, 2, experts)
    mine_terms = lax.dynamic_slice_in_dim(terms_all, place * local_experts, local_experts, axis=4)
    mine_terms = as_single(mine_terms).transpose(0, 2, 1, 3, 4)
    weights_all = jnp.sum(mine_terms, axis=3).reshape(-1, local_experts)
    packed = gather_reordered(packed_line)
    grad_line = gather_rows(after(as_half(out_grad), packed_line))
    gains = as_single(packed[:, raw_width:]).T
    gain_attn = gains[0]
    gain_ffn, rank_gains = reorder(gains[1:], 1)
    rank_gains = rank_gains.reshape(-1, shard)
    gain_query = rank_gains[:, :q_shard].reshape(-1)
    gain_key = rank_gains[:, q_shard:].reshape(-1)

    sg, su, sd = split_units(after([shared_gate, shared_up, shared_down], packed))
    grad_line = after(grad_line, sg)
    cat_gate = join_rows(expert_gate, sg)
    cat_up = join_rows(expert_up, su)
    cat_down = join_rows(expert_down, sd)
    if four_chips():
        grad_chunks = [grad_line] + [swap(grad_line, m) for m in CHIPS[1:]]

    column = jnp.arange(local_experts * expert_units + shared_gate.shape[1] // dp_count)[None, :]

    scale_in = rms_scale(block_input)
    normed_in = reorder(block_input * scale_in, 1)
    hidden_in = as_half(normed_in * gain_attn)
    raw = product(hidden_in, packed)
    query_raw = raw[:, :q_rank]
    scale_query = rms_scale(query_raw)
    normed_query = query_raw * scale_query
    query_latent = as_half(normed_query * gain_query)
    key_raw = raw[:, q_rank : q_rank + KVRANK]
    scale_key = rms_scale(key_raw)
    normed_key = key_raw * scale_key
    key_latent = as_half(normed_key * gain_key)
    own_positions = (quarter * own_rows + jnp.arange(own_rows, dtype=jnp.int32)) % SEQ
    cos_own, sin_own = angles(own_positions)
    rope_own = as_half(rotate(raw[:, q_rank + KVRANK : raw_width], cos_own, sin_own))
    latents_own = jnp.concatenate([query_latent, key_latent, rope_own], axis=1)
    latents = gather_rows(after(latents_own, grad_line))
    query_all = latents[:, :q_rank]
    key_all = latents[:, q_rank : q_rank + KVRANK]
    rope_all = latents[:, q_rank + KVRANK :]
    heads = up_q.shape[1] // (NOPE + ROPE)
    cos_all, sin_all = angles(jnp.arange(group_rows, dtype=jnp.int32) % SEQ)
    query_full = product(query_all, up_q).reshape(group_rows, heads, NOPE + ROPE)
    query_nope = as_half(query_full[..., :NOPE])
    query_rope = as_half(rotate(query_full[..., NOPE:], cos_all[:, None, :], sin_all[:, None, :]))
    key_value = as_half(product(key_all, up_kv)).reshape(group_rows, heads, NOPE + VDIM)
    key_nope = key_value[..., :NOPE]
    values = key_value[..., NOPE:]
    places = jnp.arange(SEQ, dtype=jnp.int32)
    causal = places[:, None] >= places[None, :]
    mask = causal & (segments[:, None] == segments[None, :])
    scores = score_block(query_nope, query_rope, key_nope, rope_all, mask)
    total = jax.nn.logsumexp(scores, axis=-1)
    probs = as_half(jnp.exp(scores - total[..., None]))
    mixed = jnp.einsum("hqk,khd->qhd", probs, values, preferred_element_type=jnp.float32)
    attended = as_half(mixed).reshape(group_rows, heads * VDIM)
    projected = against_rows(attended, proj_out)
    mid = block_input + scatter_rows(projected)
    scale_mid = rms_scale(mid)
    normed_mid = mid * scale_mid
    hidden_mid = as_half(normed_mid * gain_ffn)

    hidden_line = gather_rows(hidden_mid)

    def expert_block(hidden, d_act_raw, grad, mine, before=()):
        factor = jnp.ones((1, 1), jnp.float32)
        for e in range(local_experts):
            inside = (column >= e * expert_units) & (column < (e + 1) * expert_units)
            factor = jnp.where(inside, mine[:, e : e + 1], factor)
        gate_val = against_rows(hidden, cat_gate)
        hidden, gate_val = after((hidden, gate_val), before)
        up_val = against_rows(hidden, cat_up)
        d_act = d_act_raw * factor
        sigma = jax.nn.sigmoid(gate_val)
        act = as_half(gate_val * sigma * up_val)
        act = as_half(as_single(act) * factor)
        d_gate = as_half(d_act * up_val * sigma * (1.0 + gate_val * (1.0 - sigma)))
        d_up = as_half(d_act * gate_val * sigma)
        back = product(d_gate, cat_gate)
        back = as_half(back + product(d_up, cat_up))
        more = (hidden, grad, d_gate, d_up, act)
        return back, more

    def weight_grads(sums, more):
        hidden, grad, d_gate, d_up, act = more
        new = (
            contract_rows(d_gate, hidden),
            contract_rows(d_up, hidden),
            contract_rows(act, grad),
        )
        return new if sums is None else tuple(x + y for x, y in zip(sums, new))

    def sum_over(terms):
        total = terms[0]
        for term in terms[1:]:
            total = total + term
        return total

    sums = None
    act_blocks = []
    out_parts = []
    if four_chips():
        def block_weights(mask):
            far = [
                lax.dynamic_slice_in_dim(weights_all, (place ^ m) * group_rows, group_rows, axis=0)
                for m in (mask, mask | 1)
            ]
            return jnp.concatenate(far, axis=0)

        grad_chunks = after(grad_chunks, projected)
        grad_blocks = [both_cores(chunk) for chunk in grad_chunks]
        raw_blocks = [against_rows(grad, cat_down) for grad in grad_blocks]
        mine_blocks = [block_weights(m) for m in CHIPS]
        hidden_line, raw_blocks, mine_blocks = lax.optimization_barrier(
            (hidden_line, raw_blocks, mine_blocks)
        )
        half = group_rows // 2
        along = swap(hidden_line, 2)
        across = swap(hidden_line, 4)
        back, more = expert_block(
            both_cores(hidden_line), raw_blocks[0], grad_blocks[0], mine_blocks[0]
        )
        mores = [more]
        own_back = back
        along, across = after((along, across), back)
        corner = [swap(along[:half], 4), swap(across[half:], 2)]
        corner = jnp.concatenate(corner, axis=0)
        arrived = []
        before = ()
        for i, chunk in enumerate((along, across, corner), 1):
            back, more = expert_block(
                both_cores(after(chunk, back)), raw_blocks[i], grad_blocks[i], mine_blocks[i], before
            )
            mores.append(more)
            part = pair_sum(back)
            before = (part,)
            arrived.append(swap(part, CHIPS[i]))
        grad_gate = sum_over([contract_rows(more[2], more[0]) for more in mores])
        grad_up = sum_over([contract_rows(more[3], more[0]) for more in mores])
        arrived[-1], grad_gate, grad_up = lax.optimization_barrier((arrived[-1], grad_gate, grad_up))
        back_sum = add_parts([pair_sum(own_back), *arrived])
        act_blocks = [more[4] for more in mores]
    else:
        rounds = max(1, dp_count // 8)
        size = group_rows // rounds
        rounds_weights = weights_all.reshape(dp_count, rounds, size, local_experts)
        backs = []
        for i in range(rounds):
            rows = (hidden_line[i * size : (i + 1) * size], grad_line[i * size : (i + 1) * size])
            if backs:
                rows = after(rows, backs[-1], sums)
            hidden, grad = (gather_plane(r) for r in rows)
            mine = rounds_weights[:, i].reshape(-1, local_experts)
            back, more = expert_block(hidden, against_rows(grad, cat_down), grad, mine)
            sums = weight_grads(sums, more)
            act_blocks.append(more[4])
            backs.append(scatter_plane(back))
        back_sum = jnp.concatenate(backs, axis=0)
    d_hidden_mid = scatter_rows(back_sum)

    grad_gain_ffn = jnp.sum(d_hidden_mid * normed_mid, axis=0)
    d_mid = out_grad + norm_back(d_hidden_mid, normed_mid, scale_mid, gain_ffn)
    mid_low = as_half(d_mid)
    act_blocks = after(act_blocks, back_sum)
    if four_chips():
        out_parts = [pair_sum(as_half(product(act, cat_down))) for act in act_blocks]
    else:
        for act in act_blocks:
            if out_parts:
                act = after(act, out_parts[-1])
            out_parts.append(scatter_plane(as_half(product(act, cat_down))))

    mid_all = gather_rows(mid_low)
    if four_chips():
        late_acts = after(act_blocks, mid_low)
        grad_down = sum_over([contract_rows(a, g) for a, g in zip(late_acts, grad_blocks)])
        sums = (grad_gate, grad_up, grad_down)
    mid_all = after(mid_all, sums)
    shared_sums = after([as_half(g[local_experts * expert_units :]) for g in sums], mid_all)
    shared_grads = join_units(shared_sums)
    grad_proj_out = contract_rows(mid_all, attended)
    d_attended = product(mid_all, proj_out)
    d_attended = as_half(d_attended).reshape(group_rows, heads, VDIM)
    scale = 1.0 / math.sqrt(NOPE + ROPE)
    scores = score_block(query_nope, query_rope, key_nope, rope_all, mask)
    probs = jnp.exp(scores - total[..., None])
    probs_low = as_half(probs)
    value_grads = jnp.einsum(
        "hqk,qhd->khd", probs_low, d_attended, preferred_element_type=jnp.float32
    )
    d_probs = jnp.einsum("qhd,khd->hqk", d_attended, values, preferred_element_type=jnp.float32)
    delta = jnp.sum(probs * d_probs, axis=-1, keepdims=True)
    d_scores = as_half(probs * (d_probs - delta) * scale)
    query_nope_grads = jnp.einsum(
        "hqk,khd->qhd", d_scores, key_nope, preferred_element_type=jnp.float32
    )
    query_rope_grads = jnp.einsum(
        "hqk,kd->qhd", d_scores, rope_all, preferred_element_type=jnp.float32
    )
    key_nope_grads = jnp.einsum(
        "hqk,qhd->khd", d_scores, query_nope, preferred_element_type=jnp.float32
    )
    rope_key_grads = jnp.einsum(
        "hqk,qhd->kd", d_scores, query_rope, preferred_element_type=jnp.float32
    )
    d_query_rope = unrotate(query_rope_grads, cos_all[:, None, :], sin_all[:, None, :])
    d_query = as_half(jnp.concatenate([query_nope_grads, d_query_rope], axis=-1)).reshape(
        group_rows, heads * (NOPE + ROPE)
    )
    grad_up_q = contract_rows(query_all, d_query)
    d_query_latent = against_rows(d_query, up_q)
    d_key_value = as_half(jnp.concatenate([key_nope_grads, value_grads], axis=-1)).reshape(
        group_rows, heads * (NOPE + VDIM)
    )
    grad_up_kv = contract_rows(key_all, d_key_value)
    d_key_latent = against_rows(d_key_value, up_kv)
    d_latents_own = jnp.concatenate(
        [as_half(d_query_latent), as_half(d_key_latent), as_half(rope_key_grads)], axis=1
    )
    d_latents_own, shared_grads = lax.optimization_barrier((d_latents_own, shared_grads))
    d_latents = scatter_rows(d_latents_own)
    sums = after(sums, d_latents_own)
    grad_gate, grad_up, grad_down = sums

    def fold_whole(grads, index):
        width = denses[index].shape[1]
        part = as_half(grads).reshape(dp_count, times[index], base, width).transpose(0, 2, 1, 3)
        return part.reshape(dp_count * base, -1)

    dense_grads = (grad_up_q, grad_up_kv, grad_proj_out)
    folded_grads = jnp.concatenate([fold_whole(g, i) for i, g in enumerate(dense_grads)], axis=1)
    folded_grads = after(folded_grads, d_latents_own)
    if four_chips():
        dense_own = parts_of(reorder(folded_grads, 0))
        dense_parts = [send_part(p, m) for p, m in zip(dense_own, CHIPS)]
        out_parts = [send_part(p, m) for p, m in zip(out_parts, CHIPS)]
        out_sum = add_parts(out_parts)
    else:
        dense_sums = scatter_plane(folded_grads)
        out_sum = jnp.concatenate(out_parts, axis=0)
    block_output = mid + scatter_rows(after(out_sum, d_latents_own))
    latent_q = d_latents[:, :q_rank]
    latent_k = d_latents[:, q_rank : q_rank + KVRANK]
    latent_r = d_latents[:, q_rank + KVRANK :]
    grad_gain_query = jnp.sum(latent_q * normed_query, axis=0)
    d_query_raw = norm_back(latent_q, normed_query, scale_query, gain_query)
    grad_gain_key = jnp.sum(latent_k * normed_key, axis=0)
    d_key_raw = norm_back(latent_k, normed_key, scale_key, gain_key)
    d_rope_raw = unrotate(latent_r, cos_own, sin_own)
    extra = packed.shape[1] - raw_width
    d_raw = as_half(
        jnp.concatenate(
            [d_query_raw, d_key_raw, d_rope_raw, jnp.zeros((own_rows, extra), jnp.float32)], axis=1
        )
    )
    d_hidden_in = against_rows(d_raw, packed)
    grad_gain_attn = jnp.sum(d_hidden_in * normed_in, axis=0)
    input_grad = d_mid + reorder(norm_back(d_hidden_in, normed_in, scale_in, gain_attn), 1)
    rank_grads = jnp.concatenate(
        [grad_gain_query.reshape(-1, q_shard), grad_gain_key.reshape(-1, shard - q_shard)], axis=1
    ).reshape(-1)
    late_grads = reorder(jnp.stack([grad_gain_ffn, rank_grads]), 1)
    gain_grads = jnp.concatenate([grad_gain_attn[None], late_grads], axis=0).T
    packed_grads = contract_rows(hidden_in, d_raw)
    packed_grads = packed_grads + jnp.pad(gain_grads, ((0, 0), (raw_width, 0)))
    if four_chips():
        packed_parts = [send_part(p, m) for p, m in zip(parts_of(as_half(packed_grads)), CHIPS)]
        packed_sums = add_parts(packed_parts)
        dense_sums = add_parts(after(dense_parts, packed_sums))
    else:
        packed_sums = scatter_plane(as_half(packed_grads))
    down_out = scatter_rows(packed_sums)
    up_q_out, up_kv_out, proj_grad_out = (
        as_single(unfold_rows(dense_sums[:, ends[i] : ends[i + 1]], times[i])) for i in range(3)
    )
    grad_gate_sh, grad_up_sh, grad_down_sh = (as_single(g) for g in shared_grads)
    gains_out = down_out[:, raw_width:]

    routed_units = local_experts * expert_units

    def cut(grads):
        return grads[:routed_units].reshape(local_experts, expert_units, model).swapaxes(1, 2)

    return (
        block_output,
        input_grad,
        gains_out[:, 0],
        down_out[:, :q_rank],
        gains_out[:q_shard, 2],
        up_q_out,
        down_out[:, q_rank:raw_width],
        gains_out[q_shard:, 2],
        up_kv_out,
        proj_grad_out,
        gains_out[:, 1],
        grad_gate_sh,
        grad_up_sh,
        grad_down_sh,
        cut(grad_gate),
        cut(grad_up),
        cut(grad_down),
    )


def solution(mesh):
    in_specs = (
        P(("dp", "tensor"), None),
        P(("dp", "tensor"), None),
        P("dp"),
        P("dp", None),
        P("dp", None),
        P(("dp", "tensor")),
        P(("dp", "tensor"), None),
        P(("dp", "tensor")),
        P("dp", "tensor"),
        P(("dp", "tensor"), None),
        P(("dp", "tensor")),
        P("dp", "tensor"),
        P("dp", "tensor"),
        P(("dp", "tensor")),
        P("dp", "tensor"),
        P("dp", "tensor"),
        P("dp", "tensor"),
        P("dp", None, "tensor"),
        P("dp", None, "tensor"),
        P("dp", None, "tensor"),
    )
    out_specs = (
        P(("dp", "tensor"), None),
        P(("dp", "tensor"), None),
        P(("dp", "tensor")),
        P(("dp", "tensor"), None),
        P(("dp", "tensor")),
        P("dp", "tensor"),
        P(("dp", "tensor"), None),
        P(("dp", "tensor")),
        P("dp", "tensor"),
        P("dp", "tensor"),
        P(("dp", "tensor")),
        P("dp", "tensor"),
        P("dp", "tensor"),
        P("dp", "tensor"),
        P("dp", None, "tensor"),
        P("dp", None, "tensor"),
        P("dp", None, "tensor"),
    )
    return jax.shard_map(layer, mesh=mesh, in_specs=in_specs, out_specs=out_specs, check_vma=False)
```

```python
import math

import jax
import jax.numpy as jnp
from jax import lax
from jax.experimental.layout import Layout, with_layout_constraint
from jax.sharding import PartitionSpec as P

NOPE = 128
ROPE = 64
VDIM = 128
KVRANK = 512
SEQ = 512


EPS = 1e-06
THETA = 50000.0


def as_half(values):
    return values.astype(jnp.bfloat16)


def as_single(values):
    return values.astype(jnp.float32)


def product(left, right):
    return jnp.dot(left, right, preferred_element_type=jnp.float32)


def contract_rows(left, right):
    return lax.dot_general(
        left, right, (((0,), (0,)), ((), ())), preferred_element_type=jnp.float32
    )


def against_rows(left, right):
    return lax.dot_general(
        left, right, (((1,), (1,)), ((), ())), preferred_element_type=jnp.float32
    )


def rms_scale(values):
    return lax.rsqrt(jnp.mean(values * values, axis=-1, keepdims=True) + EPS)


def norm_back(grad, normed, scale, gain):
    scaled = grad * gain
    return scale * (scaled - normed * jnp.mean(scaled * normed, axis=-1, keepdims=True))


def angles(positions):
    half = ROPE // 2
    freq = THETA ** (-jnp.arange(half, dtype=jnp.float32) * 2.0 / ROPE)
    phase = as_single(positions)[:, None] * freq[None, :]
    return (jnp.cos(phase), jnp.sin(phase))


def rotate(values, cosine, sine):
    half = values.shape[-1] // 2
    first = values[..., :half]
    second = values[..., half:]
    return jnp.concatenate(
        [first * cosine - second * sine, second * cosine + first * sine], axis=-1
    )


def unrotate(values, cosine, sine):
    half = values.shape[-1] // 2
    first = values[..., :half]
    second = values[..., half:]
    return jnp.concatenate(
        [first * cosine + second * sine, second * cosine - first * sine], axis=-1
    )


def score_block(query_nope, query_rope, key_nope, rope_key, mask):
    scale = 1.0 / math.sqrt(NOPE + ROPE)
    scores = jnp.einsum("qhd,khd->hqk", query_nope, key_nope, preferred_element_type=jnp.float32)
    scores = scores + jnp.einsum(
        "qhd,kd->hqk", query_rope, rope_key, preferred_element_type=jnp.float32
    )
    return jnp.where(mask[None], scores * scale, -jnp.inf)


def after(value, *before):
    return lax.optimization_barrier((value, before))[0]


def fold_rows(rows, base):
    _, width = rows.shape
    return rows.reshape(-1, base, width).transpose(1, 0, 2).reshape(base, -1)


def unfold_rows(rows, times):
    base = rows.shape[0]
    return rows.reshape(base, times, -1).transpose(1, 0, 2).reshape(base * times, -1)


def swap(rows, mask):
    count = lax.axis_size("dp")
    return lax.ppermute(rows, "dp", [(i, i ^ mask) for i in range(count)])


def four_chips():
    return lax.axis_size("dp") == 2 * 2 * 2


def fetch_chunks(rows):
    half = rows.shape[0] // 2
    along = swap(rows, 2)
    across = swap(rows, 4)
    side = swap(rows, 1)
    first = swap(along[:half], 4)
    second = swap(across[half:], 2)
    corner = jnp.concatenate([first, second], axis=0)
    return {
        0: rows,
        1: side,
        2: along,
        3: swap(along, 1),
        4: across,
        5: swap(across, 1),
        6: corner,
        7: swap(corner, 1),
    }


CHIPS = (0, 2, 4, 6)


def both_cores(rows):
    return jnp.concatenate([rows, swap(rows, 1)], axis=0)


def pair_sum(block):
    count = block.shape[0] // 2
    return as_half(as_single(block[:count]) + as_single(swap(block[count:], 1)))


def send_part(part, mask):
    return swap(part, mask) if mask else part


def add_parts(parts):
    total = as_single(parts[0])
    for part in parts[1:]:
        total = total + as_single(part)
    return as_half(total)


def scatter_plane(block):
    return lax.psum_scatter(block, "dp", scatter_dimension=0, tiled=True)


def gather_plane(block):
    return lax.all_gather(block, "dp", axis=0, tiled=True)


def row_major(values):
    return with_layout_constraint(values, Layout(major_to_minor=(0, 1)))


def fetch_list(rows):
    if not four_chips():
        return [lax.all_gather(rows, "dp", axis=0, tiled=True)]
    chunks = fetch_chunks(rows)
    return [chunks[m] for m in range(len(chunks))]


def assemble(chunks):
    if len(chunks) == 1:
        return chunks[0]
    place = lax.axis_index("dp")
    count, width = chunks[0].shape
    whole = jnp.zeros((count * len(chunks), width), chunks[0].dtype)
    for mask, chunk in enumerate(chunks):
        whole = lax.dynamic_update_slice(whole, chunk, ((place ^ mask) * count, 0))
    return row_major(whole)


def reorder(values, axis):
    if not four_chips():
        return values
    place = lax.axis_index("dp")
    count = lax.axis_size("dp")
    size = values.shape[axis] // count
    return jnp.concatenate(
        [
            lax.dynamic_slice_in_dim(values, (place ^ m) * size, size, axis=axis)
            for m in range(count)
        ],
        axis=axis,
    )


def parts_of(rows):
    count = rows.shape[0] // lax.axis_size("dp")

    def part(mask):
        return rows[mask * count : (mask + 1) * count]

    return [
        as_half(as_single(part(m)) + as_single(swap(part(m | 1), 1))) for m in CHIPS
    ]


def gather_rows(rows):
    return lax.all_gather(rows, "tensor", axis=0, tiled=True)


def scatter_rows(rows):
    return as_single(
        lax.psum_scatter(as_half(rows), "tensor", scatter_dimension=0, tiled=True)
    )


def exchange(block):
    return lax.all_to_all(block, "dp", split_axis=0, concat_axis=0, tiled=True)


def split_units(weights):
    dp_count = lax.axis_size("dp")
    rows, units = weights[0].shape
    share = units // dp_count
    stacked = jnp.stack([w.T for w in weights]).reshape(3, dp_count, share, rows)
    stacked = stacked.transpose(1, 0, 2, 3).reshape(dp_count, 3 * share, rows)
    got = exchange(stacked).reshape(dp_count, 3, share, rows)
    return got.transpose(1, 2, 0, 3).reshape(3, share, dp_count * rows)


def join_units(grads):
    dp_count = lax.axis_size("dp")
    share, all_rows = grads[0].shape
    rows = all_rows // dp_count
    stacked = jnp.stack(grads).reshape(3, share, dp_count, rows).transpose(2, 0, 1, 3)
    got = exchange(stacked.reshape(dp_count, 3 * share, rows)).reshape(dp_count, 3, share, rows)
    return [g.T for g in got.transpose(1, 0, 2, 3).reshape(3, dp_count * share, rows)]


def pad_rows(rows):
    return jnp.pad(rows, ((0, -rows.shape[0] % 16), (0, 0)))


def join_rows(experts_weight, shared_slice):
    count, model, units = experts_weight.shape
    return jnp.concatenate(
        [experts_weight.swapaxes(1, 2).reshape(count * units, model), shared_slice], axis=0
    )


def layer(
    block_input,
    out_grad,
    segments,
    routes,
    route_weight,
    norm_attn,
    query_down,
    query_norm,
    query_up,
    latent_down,
    latent_norm,
    latent_up,
    out_proj,
    norm_ffn,
    shared_gate,
    shared_up,
    shared_down,
    expert_gate,
    expert_up,
    expert_down,
):
    dp_count = lax.axis_size("dp")
    place = lax.axis_index("dp")
    quarter = lax.axis_index("tensor")
    own_rows = block_input.shape[0]
    group_rows = segments.shape[0]
    local_experts, model, expert_units = expert_gate.shape
    experts = local_experts * dp_count
    q_rank = query_down.shape[1]
    raw_width = q_rank + latent_down.shape[1]
    shard = query_down.shape[0]
    q_shard = query_norm.shape[0]

    packed_own = jnp.concatenate(
        [
            query_down,
            latent_down,
            norm_attn[:, None],
            norm_ffn[:, None],
            jnp.concatenate([query_norm, latent_norm])[:, None],
        ],
        axis=1,
    )
    packed_line = gather_rows(packed_own)
    base = latent_up.shape[0]
    denses = (query_up, latent_up, out_proj)
    times = [w.shape[0] // base for w in denses]
    ends = [0]
    for w in denses:
        ends.append(ends[-1] + w.size // base)
    chosen = routes[:, :, None] == jnp.arange(experts, dtype=jnp.int32)[None, None, :]
    dense_weight = jnp.sum(jnp.where(chosen, route_weight[:, :, None], 0.0), axis=1)
    upper = as_half(dense_weight)
    terms = jnp.concatenate([upper, as_half(dense_weight - as_single(upper))], axis=1)
    folds = [fold_rows(w, base) for w in (*denses, terms)]
    folded_chunks = fetch_list(jnp.concatenate(after(folds, packed_own), axis=1))

    def unfold_whole(index):
        part = folded[:, ends[index] : ends[index + 1]]
        width = denses[index].shape[1]
        part = part.reshape(dp_count, base, times[index], width).transpose(0, 2, 1, 3)
        return part.reshape(-1, width)

    packed_line, folded_chunks = lax.optimization_barrier((packed_line, folded_chunks))
    packed_chunks = fetch_list(row_major(packed_line))
    folded = assemble(folded_chunks)
    up_q, up_kv, proj_out = (unfold_whole(i) for i in range(3))
    terms_all = folded[:, ends[3] :].reshape(dp_count, base, group_rows // base, 2, experts)
    mine_terms = lax.dynamic_slice_in_dim(terms_all, place * local_experts, local_experts, axis=4)
    mine_terms = as_single(mine_terms).transpose(0, 2, 1, 3, 4)
    weights_all = jnp.sum(mine_terms, axis=3).reshape(-1, local_experts)
    grad_line = gather_rows(after(as_half(out_grad), packed_line))
    grad_sent = after(grad_line, packed_chunks)
    shared_units = split_units(after([shared_gate, shared_up, shared_down], packed_chunks))
    if four_chips():
        grad_chunks = [grad_sent] + [swap(grad_sent, m) for m in CHIPS[1:]]

    scale_in = rms_scale(block_input)
    normed_in = reorder(block_input * scale_in, 1)
    raw = None
    hidden_pieces = []
    gain_pieces = []
    for i, chunk in enumerate(packed_chunks):
        size = chunk.shape[0]
        normed_piece = normed_in[:, i * size : (i + 1) * size]
        chunk, normed_piece = lax.optimization_barrier((chunk, normed_piece))
        piece_gains = as_single(chunk[:, raw_width:]).T
        piece = as_half(normed_piece * piece_gains[0])
        more = product(piece, chunk)
        raw = more if raw is None else raw + more
        hidden_pieces.append(piece)
        gain_pieces.append(piece_gains)
    late_gains = gain_pieces[0][1:]
    if four_chips():
        late_gains = jnp.zeros((2, model), jnp.float32)
        for mask, piece_gains in enumerate(gain_pieces):
            late_gains = lax.dynamic_update_slice(
                late_gains, piece_gains[1:], (0, (place ^ mask) * piece_gains.shape[1])
            )
    gain_ffn, rank_gains = late_gains
    rank_gains = rank_gains.reshape(-1, shard)
    gain_query = rank_gains[:, :q_shard].reshape(-1)
    gain_key = rank_gains[:, q_shard:].reshape(-1)
    query_raw = raw[:, :q_rank]
    scale_query = rms_scale(query_raw)
    normed_query = query_raw * scale_query
    query_latent = as_half(normed_query * gain_query)
    key_raw = raw[:, q_rank : q_rank + KVRANK]
    scale_key = rms_scale(key_raw)
    normed_key = key_raw * scale_key
    key_latent = as_half(normed_key * gain_key)
    own_positions = (quarter * own_rows + jnp.arange(own_rows, dtype=jnp.int32)) % SEQ
    cos_own, sin_own = angles(own_positions)
    rope_own = as_half(rotate(raw[:, q_rank + KVRANK : raw_width], cos_own, sin_own))
    latents_own = jnp.concatenate([query_latent, key_latent, rope_own], axis=1)
    latents = gather_rows(after(latents_own, grad_line))
    hidden_in = jnp.concatenate(after(hidden_pieces, latents_own), axis=1)
    packed = jnp.concatenate(after(packed_chunks, latents_own), axis=0)
    gain_attn = jnp.concatenate([g[0] for g in after(gain_pieces, latents_own)])
    query_all = latents[:, :q_rank]
    key_all = latents[:, q_rank : q_rank + KVRANK]
    rope_all = latents[:, q_rank + KVRANK :]
    heads = up_q.shape[1] // (NOPE + ROPE)
    cos_all, sin_all = angles(jnp.arange(group_rows, dtype=jnp.int32) % SEQ)
    query_full = product(query_all, up_q).reshape(group_rows, heads, NOPE + ROPE)
    query_nope = as_half(query_full[..., :NOPE])
    query_rope = as_half(rotate(query_full[..., NOPE:], cos_all[:, None, :], sin_all[:, None, :]))
    key_value = as_half(product(key_all, up_kv)).reshape(group_rows, heads, NOPE + VDIM)
    key_nope = key_value[..., :NOPE]
    values = key_value[..., NOPE:]
    places = jnp.arange(SEQ, dtype=jnp.int32)
    causal = places[:, None] >= places[None, :]
    mask = causal & (segments[:, None] == segments[None, :])
    scores = score_block(query_nope, query_rope, key_nope, rope_all, mask)
    total = jax.nn.logsumexp(scores, axis=-1)
    probs = as_half(jnp.exp(scores - total[..., None]))
    mixed = jnp.einsum("hqk,khd->qhd", probs, values, preferred_element_type=jnp.float32)
    attended = as_half(mixed).reshape(group_rows, heads * VDIM)
    projected = against_rows(attended, proj_out)
    mid = block_input + scatter_rows(projected)
    sg, su, sd = (pad_rows(w) for w in after(shared_units, projected))
    cat_gate = join_rows(expert_gate, sg)
    cat_up = join_rows(expert_up, su)
    cat_down = join_rows(expert_down, sd)
    cat_both = jnp.concatenate([cat_gate, cat_up], axis=0)
    column = jnp.arange(cat_gate.shape[0])[None, :]
    scale_mid = rms_scale(mid)
    normed_mid = mid * scale_mid
    hidden_mid = as_half(normed_mid * gain_ffn)

    hidden_line = gather_rows(hidden_mid)

    def expert_block(hidden, d_act_raw, grad, mine, before=()):
        factor = jnp.ones((1, 1), jnp.float32)
        for e in range(local_experts):
            inside = (column >= e * expert_units) & (column < (e + 1) * expert_units)
            factor = jnp.where(inside, mine[:, e : e + 1], factor)
        gate_val = against_rows(hidden, cat_gate)
        hidden, gate_val = after((hidden, gate_val), before)
        up_val = against_rows(hidden, cat_up)
        d_act = d_act_raw * factor
        sigma = jax.nn.sigmoid(gate_val)
        act = as_half(gate_val * sigma * up_val)
        act = as_half(as_single(act) * factor)
        d_gate = as_half(d_act * up_val * sigma * (1.0 + gate_val * (1.0 - sigma)))
        d_up = as_half(d_act * gate_val * sigma)
        back = product(jnp.concatenate([d_gate, d_up], axis=1), cat_both)
        back = as_half(back)
        more = (hidden, grad, d_gate, d_up, act)
        return back, more

    def weight_grads(sums, more):
        hidden, grad, d_gate, d_up, act = more
        new = (
            contract_rows(d_gate, hidden),
            contract_rows(d_up, hidden),
            contract_rows(act, grad),
        )
        return new if sums is None else tuple(x + y for x, y in zip(sums, new))

    def sum_over(terms):
        total = terms[0]
        for term in terms[1:]:
            total = total + term
        return total

    sums = None
    act_blocks = []
    out_parts = []
    if four_chips():
        def block_weights(mask):
            far = [
                lax.dynamic_slice_in_dim(weights_all, (place ^ m) * group_rows, group_rows, axis=0)
                for m in (mask, mask | 1)
            ]
            return jnp.concatenate(far, axis=0)

        grad_chunks = after(grad_chunks, projected)
        grad_blocks = [both_cores(chunk) for chunk in grad_chunks]
        raw_blocks = [against_rows(grad, cat_down) for grad in grad_blocks]
        mine_blocks = [block_weights(m) for m in CHIPS]
        hidden_line, raw_blocks, mine_blocks = lax.optimization_barrier(
            (hidden_line, raw_blocks, mine_blocks)
        )
        half = group_rows // 2
        along = swap(hidden_line, 2)
        across = swap(hidden_line, 4)
        back, more = expert_block(
            both_cores(hidden_line), raw_blocks[0], grad_blocks[0], mine_blocks[0]
        )
        mores = [more]
        own_back = back
        along, across = after((along, across), back)
        corner = [swap(along[:half], 4), swap(across[half:], 2)]
        corner = jnp.concatenate(corner, axis=0)
        arrived = []
        before = ()
        for i, chunk in enumerate((along, across, corner), 1):
            back, more = expert_block(
                both_cores(after(chunk, back)), raw_blocks[i], grad_blocks[i], mine_blocks[i], before
            )
            mores.append(more)
            part = pair_sum(back)
            before = (part,)
            arrived.append(swap(part, CHIPS[i]))
        grad_gate = sum_over([contract_rows(more[2], more[0]) for more in mores])
        grad_up = sum_over([contract_rows(more[3], more[0]) for more in mores])
        arrived[-1], grad_gate, grad_up = lax.optimization_barrier((arrived[-1], grad_gate, grad_up))
        back_sum = add_parts([pair_sum(own_back), *arrived])
        act_blocks = [more[4] for more in mores]
    else:
        rounds = max(1, dp_count // 8)
        size = group_rows // rounds
        rounds_weights = weights_all.reshape(dp_count, rounds, size, local_experts)
        backs = []
        for i in range(rounds):
            rows = (hidden_line[i * size : (i + 1) * size], grad_line[i * size : (i + 1) * size])
            if backs:
                rows = after(rows, backs[-1], sums)
            hidden, grad = (gather_plane(r) for r in rows)
            mine = rounds_weights[:, i].reshape(-1, local_experts)
            back, more = expert_block(hidden, against_rows(grad, cat_down), grad, mine)
            sums = weight_grads(sums, more)
            act_blocks.append(more[4])
            backs.append(scatter_plane(back))
        back_sum = jnp.concatenate(backs, axis=0)
    d_hidden_mid = scatter_rows(back_sum)

    grad_gain_ffn = jnp.sum(d_hidden_mid * normed_mid, axis=0)
    d_mid = out_grad + norm_back(d_hidden_mid, normed_mid, scale_mid, gain_ffn)
    mid_low = as_half(d_mid)
    act_blocks = after(act_blocks, back_sum)
    if four_chips():
        out_parts = [pair_sum(as_half(product(act, cat_down))) for act in act_blocks]
    else:
        for act in act_blocks:
            if out_parts:
                act = after(act, out_parts[-1])
            out_parts.append(scatter_plane(as_half(product(act, cat_down))))

    mid_all = gather_rows(mid_low)
    if four_chips():
        late_acts = after(act_blocks, mid_low)
        grad_down = sum_over([contract_rows(a, g) for a, g in zip(late_acts, grad_blocks)])
        sums = (grad_gate, grad_up, grad_down)
    mid_all = after(mid_all, sums)
    first_shared = local_experts * expert_units
    share = shared_units[0].shape[0]
    shared_sums = [as_half(g[first_shared : first_shared + share]) for g in sums]
    grad_proj_out = contract_rows(mid_all, attended)
    d_attended = product(mid_all, proj_out)
    d_attended = as_half(d_attended).reshape(group_rows, heads, VDIM)
    scale = 1.0 / math.sqrt(NOPE + ROPE)
    scores = score_block(query_nope, query_rope, key_nope, rope_all, mask)
    probs = jnp.exp(scores - total[..., None])
    probs_low = as_half(probs)
    value_grads = jnp.einsum(
        "hqk,qhd->khd", probs_low, d_attended, preferred_element_type=jnp.float32
    )
    d_probs = jnp.einsum("qhd,khd->hqk", d_attended, values, preferred_element_type=jnp.float32)
    delta = jnp.sum(probs * d_probs, axis=-1, keepdims=True)
    d_scores = as_half(probs * (d_probs - delta) * scale)
    query_nope_grads = jnp.einsum(
        "hqk,khd->qhd", d_scores, key_nope, preferred_element_type=jnp.float32
    )
    query_rope_grads = jnp.einsum(
        "hqk,kd->qhd", d_scores, rope_all, preferred_element_type=jnp.float32
    )
    key_nope_grads = jnp.einsum(
        "hqk,qhd->khd", d_scores, query_nope, preferred_element_type=jnp.float32
    )
    rope_key_grads = jnp.einsum(
        "hqk,qhd->kd", d_scores, query_rope, preferred_element_type=jnp.float32
    )
    d_query_rope = unrotate(query_rope_grads, cos_all[:, None, :], sin_all[:, None, :])
    d_query = as_half(jnp.concatenate([query_nope_grads, d_query_rope], axis=-1)).reshape(
        group_rows, heads * (NOPE + ROPE)
    )
    grad_up_q = contract_rows(query_all, d_query)
    d_query_latent = against_rows(d_query, up_q)
    d_key_value = as_half(jnp.concatenate([key_nope_grads, value_grads], axis=-1)).reshape(
        group_rows, heads * (NOPE + VDIM)
    )
    grad_up_kv = contract_rows(key_all, d_key_value)
    d_key_latent = against_rows(d_key_value, up_kv)
    d_latents_own = jnp.concatenate(
        [as_half(d_query_latent), as_half(d_key_latent), as_half(rope_key_grads)], axis=1
    )
    shared_grads = join_units(after(shared_sums, d_latents_own))
    d_latents = scatter_rows(d_latents_own)
    d_latents, shared_grads = lax.optimization_barrier((d_latents, shared_grads))
    sums = after(sums, d_latents_own)
    grad_gate, grad_up, grad_down = sums

    def fold_whole(grads, index):
        width = denses[index].shape[1]
        part = as_half(grads).reshape(dp_count, times[index], base, width).transpose(0, 2, 1, 3)
        return part.reshape(dp_count * base, -1)

    dense_grads = (grad_up_q, grad_up_kv, grad_proj_out)
    folded_grads = jnp.concatenate([fold_whole(g, i) for i, g in enumerate(dense_grads)], axis=1)
    folded_grads = after(folded_grads, d_latents_own)
    if four_chips():
        dense_own = parts_of(reorder(folded_grads, 0))
        dense_parts = [send_part(p, m) for p, m in zip(dense_own, CHIPS)]
        out_parts = [send_part(p, m) for p, m in zip(out_parts, CHIPS)]
        out_sum = add_parts(out_parts)
    else:
        dense_sums = scatter_plane(folded_grads)
        out_sum = jnp.concatenate(out_parts, axis=0)
    block_output = mid + scatter_rows(after(out_sum, d_latents_own))
    latent_q = d_latents[:, :q_rank]
    latent_k = d_latents[:, q_rank : q_rank + KVRANK]
    latent_r = d_latents[:, q_rank + KVRANK :]
    grad_gain_query = jnp.sum(latent_q * normed_query, axis=0)
    d_query_raw = norm_back(latent_q, normed_query, scale_query, gain_query)
    grad_gain_key = jnp.sum(latent_k * normed_key, axis=0)
    d_key_raw = norm_back(latent_k, normed_key, scale_key, gain_key)
    d_rope_raw = unrotate(latent_r, cos_own, sin_own)
    extra = packed.shape[1] - raw_width
    d_raw = as_half(
        jnp.concatenate(
            [d_query_raw, d_key_raw, d_rope_raw, jnp.zeros((own_rows, extra), jnp.float32)], axis=1
        )
    )
    d_hidden_in = against_rows(d_raw, packed)
    grad_gain_attn = jnp.sum(d_hidden_in * normed_in, axis=0)
    input_grad = d_mid + reorder(norm_back(d_hidden_in, normed_in, scale_in, gain_attn), 1)
    rank_grads = jnp.concatenate(
        [grad_gain_query.reshape(-1, q_shard), grad_gain_key.reshape(-1, shard - q_shard)], axis=1
    ).reshape(-1)
    late_grads = reorder(jnp.stack([grad_gain_ffn, rank_grads]), 1)
    gain_grads = jnp.concatenate([grad_gain_attn[None], late_grads], axis=0).T
    packed_grads = contract_rows(hidden_in, d_raw)
    packed_grads = packed_grads + jnp.pad(gain_grads, ((0, 0), (raw_width, 0)))
    if four_chips():
        packed_parts = [send_part(p, m) for p, m in zip(parts_of(as_half(packed_grads)), CHIPS)]
        packed_sums = add_parts(packed_parts)
        dense_sums = add_parts(after(dense_parts, packed_sums))
    else:
        packed_sums = scatter_plane(as_half(packed_grads))
    down_out = scatter_rows(packed_sums)
    up_q_out, up_kv_out, proj_grad_out = (
        as_single(unfold_rows(dense_sums[:, ends[i] : ends[i + 1]], times[i])) for i in range(3)
    )
    grad_gate_sh, grad_up_sh, grad_down_sh = (as_single(g) for g in shared_grads)
    gains_out = down_out[:, raw_width:]

    routed_units = local_experts * expert_units

    def cut(grads):
        return grads[:routed_units].reshape(local_experts, expert_units, model).swapaxes(1, 2)

    return (
        block_output,
        input_grad,
        gains_out[:, 0],
        down_out[:, :q_rank],
        gains_out[:q_shard, 2],
        up_q_out,
        down_out[:, q_rank:raw_width],
        gains_out[q_shard:, 2],
        up_kv_out,
        proj_grad_out,
        gains_out[:, 1],
        grad_gate_sh,
        grad_up_sh,
        grad_down_sh,
        cut(grad_gate),
        cut(grad_up),
        cut(grad_down),
    )


def solution(mesh):
    in_specs = (
        P(("dp", "tensor"), None),
        P(("dp", "tensor"), None),
        P("dp"),
        P("dp", None),
        P("dp", None),
        P(("dp", "tensor")),
        P(("dp", "tensor"), None),
        P(("dp", "tensor")),
        P("dp", "tensor"),
        P(("dp", "tensor"), None),
        P(("dp", "tensor")),
        P("dp", "tensor"),
        P("dp", "tensor"),
        P(("dp", "tensor")),
        P("dp", "tensor"),
        P("dp", "tensor"),
        P("dp", "tensor"),
        P("dp", None, "tensor"),
        P("dp", None, "tensor"),
        P("dp", None, "tensor"),
    )
    out_specs = (
        P(("dp", "tensor"), None),
        P(("dp", "tensor"), None),
        P(("dp", "tensor")),
        P(("dp", "tensor"), None),
        P(("dp", "tensor")),
        P("dp", "tensor"),
        P(("dp", "tensor"), None),
        P(("dp", "tensor")),
        P("dp", "tensor"),
        P("dp", "tensor"),
        P(("dp", "tensor")),
        P("dp", "tensor"),
        P("dp", "tensor"),
        P("dp", "tensor"),
        P("dp", None, "tensor"),
        P("dp", None, "tensor"),
        P("dp", None, "tensor"),
    )
    return jax.shard_map(layer, mesh=mesh, in_specs=in_specs, out_specs=out_specs, check_vma=False)
```

```python
import math

import jax
import jax.numpy as jnp
from jax import lax
from jax.experimental.layout import Layout, with_layout_constraint
from jax.sharding import PartitionSpec as P

NOPE = 128
ROPE = 64
VDIM = 128
KVRANK = 512
SEQ = 512


EPS = 1e-06
THETA = 50000.0


def as_half(values):
    return values.astype(jnp.bfloat16)


def as_single(values):
    return values.astype(jnp.float32)


def product(left, right):
    return jnp.dot(left, right, preferred_element_type=jnp.float32)


def contract_rows(left, right):
    return lax.dot_general(
        left, right, (((0,), (0,)), ((), ())), preferred_element_type=jnp.float32
    )


def against_rows(left, right):
    return lax.dot_general(
        left, right, (((1,), (1,)), ((), ())), preferred_element_type=jnp.float32
    )


def rms_scale(values):
    return lax.rsqrt(jnp.mean(values * values, axis=-1, keepdims=True) + EPS)


def norm_back(grad, normed, scale, gain):
    scaled = grad * gain
    return scale * (scaled - normed * jnp.mean(scaled * normed, axis=-1, keepdims=True))


def angles(positions):
    half = ROPE // 2
    freq = THETA ** (-jnp.arange(half, dtype=jnp.float32) * 2.0 / ROPE)
    phase = as_single(positions)[:, None] * freq[None, :]
    return (jnp.cos(phase), jnp.sin(phase))


def rotate(values, cosine, sine):
    half = values.shape[-1] // 2
    first = values[..., :half]
    second = values[..., half:]
    return jnp.concatenate(
        [first * cosine - second * sine, second * cosine + first * sine], axis=-1
    )


def unrotate(values, cosine, sine):
    half = values.shape[-1] // 2
    first = values[..., :half]
    second = values[..., half:]
    return jnp.concatenate(
        [first * cosine + second * sine, second * cosine - first * sine], axis=-1
    )


def score_block(query_nope, query_rope, key_nope, rope_key, mask):
    scale = 1.0 / math.sqrt(NOPE + ROPE)
    scores = jnp.einsum("qhd,khd->hqk", query_nope, key_nope, preferred_element_type=jnp.float32)
    scores = scores + jnp.einsum(
        "qhd,kd->hqk", query_rope, rope_key, preferred_element_type=jnp.float32
    )
    return jnp.where(mask[None], scores * scale, -jnp.inf)


def after(value, *before):
    return lax.optimization_barrier((value, before))[0]


def fold_rows(rows, base):
    _, width = rows.shape
    return rows.reshape(-1, base, width).transpose(1, 0, 2).reshape(base, -1)


def unfold_rows(rows, times):
    base = rows.shape[0]
    return rows.reshape(base, times, -1).transpose(1, 0, 2).reshape(base * times, -1)


def swap(rows, mask):
    count = lax.axis_size("dp")
    return lax.ppermute(rows, "dp", [(i, i ^ mask) for i in range(count)])


def four_chips():
    return lax.axis_size("dp") == 2 * 2 * 2


def fetch_chunks(rows):
    half = rows.shape[0] // 2
    along = swap(rows, 2)
    across = swap(rows, 4)
    side = swap(rows, 1)
    first = swap(along[:half], 4)
    second = swap(across[half:], 2)
    corner = jnp.concatenate([first, second], axis=0)
    return {
        0: rows,
        1: side,
        2: along,
        3: swap(along, 1),
        4: across,
        5: swap(across, 1),
        6: corner,
        7: swap(corner, 1),
    }


CHIPS = (0, 2, 4, 6)


def both_cores(rows):
    return jnp.concatenate([rows, swap(rows, 1)], axis=0)


def pair_sum(block):
    count = block.shape[0] // 2
    return as_half(as_single(block[:count]) + as_single(swap(block[count:], 1)))


def send_part(part, mask):
    return swap(part, mask) if mask else part


def add_parts(parts):
    total = as_single(parts[0])
    for part in parts[1:]:
        total = total + as_single(part)
    return as_half(total)


def scatter_plane(block):
    return lax.psum_scatter(block, "dp", scatter_dimension=0, tiled=True)


def gather_plane(block):
    return lax.all_gather(block, "dp", axis=0, tiled=True)


def row_major(values):
    return with_layout_constraint(values, Layout(major_to_minor=(0, 1)))


def fetch_list(rows):
    if not four_chips():
        return [lax.all_gather(rows, "dp", axis=0, tiled=True)]
    chunks = fetch_chunks(rows)
    return [chunks[m] for m in range(len(chunks))]


def assemble(chunks):
    if len(chunks) == 1:
        return chunks[0]
    place = lax.axis_index("dp")
    count, width = chunks[0].shape
    whole = jnp.zeros((count * len(chunks), width), chunks[0].dtype)
    for mask, chunk in enumerate(chunks):
        whole = lax.dynamic_update_slice(whole, chunk, ((place ^ mask) * count, 0))
    return row_major(whole)


def reorder(values, axis):
    if not four_chips():
        return values
    place = lax.axis_index("dp")
    count = lax.axis_size("dp")
    size = values.shape[axis] // count
    return jnp.concatenate(
        [
            lax.dynamic_slice_in_dim(values, (place ^ m) * size, size, axis=axis)
            for m in range(count)
        ],
        axis=axis,
    )


def parts_of(rows):
    count = rows.shape[0] // lax.axis_size("dp")

    def part(mask):
        return rows[mask * count : (mask + 1) * count]

    return [
        as_half(as_single(part(m)) + as_single(swap(part(m | 1), 1))) for m in CHIPS
    ]


def gather_rows(rows):
    return lax.all_gather(rows, "tensor", axis=0, tiled=True)


def scatter_rows(rows):
    return as_single(
        lax.psum_scatter(as_half(rows), "tensor", scatter_dimension=0, tiled=True)
    )


def exchange(block):
    return lax.all_to_all(block, "dp", split_axis=0, concat_axis=0, tiled=True)


def split_units(weights):
    dp_count = lax.axis_size("dp")
    rows, units = weights[0].shape
    share = units // dp_count
    stacked = jnp.stack([w.T for w in weights]).reshape(3, dp_count, share, rows)
    stacked = stacked.transpose(1, 0, 2, 3).reshape(dp_count, 3 * share, rows)
    got = exchange(stacked).reshape(dp_count, 3, share, rows)
    return got.transpose(1, 2, 0, 3).reshape(3, share, dp_count * rows)


def join_units(grads):
    dp_count = lax.axis_size("dp")
    share, all_rows = grads[0].shape
    rows = all_rows // dp_count
    stacked = jnp.stack(grads).reshape(3, share, dp_count, rows).transpose(2, 0, 1, 3)
    got = exchange(stacked.reshape(dp_count, 3 * share, rows)).reshape(dp_count, 3, share, rows)
    return [g.T for g in got.transpose(1, 0, 2, 3).reshape(3, dp_count * share, rows)]


def pad_rows(rows):
    return jnp.pad(rows, ((0, -rows.shape[0] % 16), (0, 0)))


def join_rows(experts_weight, shared_slice):
    count, model, units = experts_weight.shape
    return jnp.concatenate(
        [experts_weight.swapaxes(1, 2).reshape(count * units, model), shared_slice], axis=0
    )


def layer(
    block_input,
    out_grad,
    segments,
    routes,
    route_weight,
    norm_attn,
    query_down,
    query_norm,
    query_up,
    latent_down,
    latent_norm,
    latent_up,
    out_proj,
    norm_ffn,
    shared_gate,
    shared_up,
    shared_down,
    expert_gate,
    expert_up,
    expert_down,
):
    dp_count = lax.axis_size("dp")
    place = lax.axis_index("dp")
    quarter = lax.axis_index("tensor")
    own_rows = block_input.shape[0]
    group_rows = segments.shape[0]
    local_experts, model, expert_units = expert_gate.shape
    experts = local_experts * dp_count
    q_rank = query_down.shape[1]
    raw_width = q_rank + latent_down.shape[1]
    shard = query_down.shape[0]
    q_shard = query_norm.shape[0]

    packed_own = jnp.concatenate(
        [
            query_down,
            latent_down,
            norm_attn[:, None],
            norm_ffn[:, None],
            jnp.concatenate([query_norm, latent_norm])[:, None],
        ],
        axis=1,
    )
    packed_line = gather_rows(packed_own)
    base = latent_up.shape[0]
    denses = (query_up, latent_up, out_proj)
    times = [w.shape[0] // base for w in denses]
    ends = [0]
    for w in denses:
        ends.append(ends[-1] + w.size // base)
    chosen = routes[:, :, None] == jnp.arange(experts, dtype=jnp.int32)[None, None, :]
    dense_weight = jnp.sum(jnp.where(chosen, route_weight[:, :, None], 0.0), axis=1)
    upper = as_half(dense_weight)
    terms = jnp.concatenate([upper, as_half(dense_weight - as_single(upper))], axis=1)
    folds = [fold_rows(w, base) for w in (*denses, terms)]
    folded_chunks = fetch_list(jnp.concatenate(after(folds, packed_own), axis=1))

    def unfold_whole(index):
        part = folded[:, ends[index] : ends[index + 1]]
        width = denses[index].shape[1]
        part = part.reshape(dp_count, base, times[index], width).transpose(0, 2, 1, 3)
        return part.reshape(-1, width)

    packed_line, folded_chunks = lax.optimization_barrier((packed_line, folded_chunks))
    packed_chunks = fetch_list(row_major(packed_line))
    folded = assemble(folded_chunks)
    up_q, up_kv, proj_out = (unfold_whole(i) for i in range(3))
    terms_all = folded[:, ends[3] :].reshape(dp_count, base, group_rows // base, 2, experts)
    mine_terms = lax.dynamic_slice_in_dim(terms_all, place * local_experts, local_experts, axis=4)
    mine_terms = as_single(mine_terms).transpose(0, 2, 1, 3, 4)
    weights_all = jnp.sum(mine_terms, axis=3).reshape(-1, local_experts)
    grad_line = gather_rows(after(as_half(out_grad), packed_line))
    grad_sent = after(grad_line, packed_chunks)
    shared_units = split_units(after([shared_gate, shared_up, shared_down], packed_chunks))
    if four_chips():
        grad_chunks = [grad_sent] + [swap(grad_sent, m) for m in CHIPS[1:]]

    scale_in = rms_scale(block_input)
    normed_in = reorder(block_input * scale_in, 1)
    raw = None
    hidden_pieces = []
    gain_pieces = []
    for i, chunk in enumerate(packed_chunks):
        size = chunk.shape[0]
        normed_piece = normed_in[:, i * size : (i + 1) * size]
        chunk, normed_piece = lax.optimization_barrier((chunk, normed_piece))
        piece_gains = as_single(chunk[:, raw_width:]).T
        piece = as_half(normed_piece * piece_gains[0])
        more = product(piece, chunk)
        raw = more if raw is None else raw + more
        hidden_pieces.append(piece)
        gain_pieces.append(piece_gains)
    late_gains = gain_pieces[0][1:]
    if four_chips():
        late_gains = jnp.zeros((2, model), jnp.float32)
        for mask, piece_gains in enumerate(gain_pieces):
            late_gains = lax.dynamic_update_slice(
                late_gains, piece_gains[1:], (0, (place ^ mask) * piece_gains.shape[1])
            )
    gain_ffn, rank_gains = late_gains
    rank_gains = rank_gains.reshape(-1, shard)
    gain_query = rank_gains[:, :q_shard].reshape(-1)
    gain_key = rank_gains[:, q_shard:].reshape(-1)
    query_raw = raw[:, :q_rank]
    scale_query = rms_scale(query_raw)
    normed_query = query_raw * scale_query
    query_latent = as_half(normed_query * gain_query)
    key_raw = raw[:, q_rank : q_rank + KVRANK]
    scale_key = rms_scale(key_raw)
    normed_key = key_raw * scale_key
    key_latent = as_half(normed_key * gain_key)
    own_positions = (quarter * own_rows + jnp.arange(own_rows, dtype=jnp.int32)) % SEQ
    cos_own, sin_own = angles(own_positions)
    rope_own = as_half(rotate(raw[:, q_rank + KVRANK : raw_width], cos_own, sin_own))
    latents_own = jnp.concatenate([query_latent, key_latent, rope_own], axis=1)
    latents = gather_rows(after(latents_own, grad_line))
    hidden_in = jnp.concatenate(after(hidden_pieces, latents_own), axis=1)
    packed = jnp.concatenate(after(packed_chunks, latents_own), axis=0)
    gain_attn = jnp.concatenate([g[0] for g in after(gain_pieces, latents_own)])
    query_all = latents[:, :q_rank]
    key_all = latents[:, q_rank : q_rank + KVRANK]
    rope_all = latents[:, q_rank + KVRANK :]
    heads = up_q.shape[1] // (NOPE + ROPE)
    cos_all, sin_all = angles(jnp.arange(group_rows, dtype=jnp.int32) % SEQ)
    query_full = product(query_all, up_q).reshape(group_rows, heads, NOPE + ROPE)
    query_nope = as_half(query_full[..., :NOPE])
    query_rope = as_half(rotate(query_full[..., NOPE:], cos_all[:, None, :], sin_all[:, None, :]))
    key_value = as_half(product(key_all, up_kv)).reshape(group_rows, heads, NOPE + VDIM)
    key_nope = key_value[..., :NOPE]
    values = key_value[..., NOPE:]
    places = jnp.arange(SEQ, dtype=jnp.int32)
    causal = places[:, None] >= places[None, :]
    mask = causal & (segments[:, None] == segments[None, :])
    scores = score_block(query_nope, query_rope, key_nope, rope_all, mask)
    total = jax.nn.logsumexp(scores, axis=-1)
    probs = as_half(jnp.exp(scores - total[..., None]))
    mixed = jnp.einsum("hqk,khd->qhd", probs, values, preferred_element_type=jnp.float32)
    attended = as_half(mixed).reshape(group_rows, heads * VDIM)
    projected = against_rows(attended, proj_out)
    mid_sum = scatter_rows(projected)
    mid_sum, packed, gain_attn, hidden_in = lax.optimization_barrier(
        (mid_sum, packed, gain_attn, hidden_in)
    )
    mid = block_input + mid_sum
    sg, su, sd = (pad_rows(w) for w in after(shared_units, projected))
    cat_gate = join_rows(expert_gate, sg)
    cat_up = join_rows(expert_up, su)
    cat_down = join_rows(expert_down, sd)
    cat_both = jnp.concatenate([cat_gate, cat_up], axis=0)
    column = jnp.arange(cat_gate.shape[0])[None, :]
    scale_mid = rms_scale(mid)
    normed_mid = mid * scale_mid
    hidden_mid = as_half(normed_mid * gain_ffn)

    hidden_line = gather_rows(hidden_mid)

    def expert_block(hidden, d_act_raw, grad, mine, before=()):
        factor = jnp.ones((1, 1), jnp.float32)
        for e in range(local_experts):
            inside = (column >= e * expert_units) & (column < (e + 1) * expert_units)
            factor = jnp.where(inside, mine[:, e : e + 1], factor)
        gate_val = against_rows(hidden, cat_gate)
        hidden, gate_val = after((hidden, gate_val), before)
        up_val = against_rows(hidden, cat_up)
        d_act = d_act_raw * factor
        sigma = jax.nn.sigmoid(gate_val)
        act = as_half(gate_val * sigma * up_val)
        act = as_half(as_single(act) * factor)
        d_gate = as_half(d_act * up_val * sigma * (1.0 + gate_val * (1.0 - sigma)))
        d_up = as_half(d_act * gate_val * sigma)
        back = product(jnp.concatenate([d_gate, d_up], axis=1), cat_both)
        back = as_half(back)
        more = (hidden, grad, d_gate, d_up, act)
        return back, more

    def weight_grads(sums, more):
        hidden, grad, d_gate, d_up, act = more
        new = (
            contract_rows(d_gate, hidden),
            contract_rows(d_up, hidden),
            contract_rows(act, grad),
        )
        return new if sums is None else tuple(x + y for x, y in zip(sums, new))

    def sum_over(terms):
        total = terms[0]
        for term in terms[1:]:
            total = total + term
        return total

    sums = None
    act_blocks = []
    out_parts = []
    if four_chips():
        def block_weights(mask):
            far = [
                lax.dynamic_slice_in_dim(weights_all, (place ^ m) * group_rows, group_rows, axis=0)
                for m in (mask, mask | 1)
            ]
            return jnp.concatenate(far, axis=0)

        grad_chunks = after(grad_chunks, projected)
        grad_blocks = [both_cores(chunk) for chunk in grad_chunks]
        raw_blocks = [against_rows(grad, cat_down) for grad in grad_blocks]
        mine_blocks = [block_weights(m) for m in CHIPS]
        hidden_line, raw_blocks, mine_blocks = lax.optimization_barrier(
            (hidden_line, raw_blocks, mine_blocks)
        )
        half = group_rows // 2
        along = swap(hidden_line, 2)
        across = swap(hidden_line, 4)
        back, more = expert_block(
            both_cores(hidden_line), raw_blocks[0], grad_blocks[0], mine_blocks[0]
        )
        mores = [more]
        own_back = back
        along, across = after((along, across), back)
        corner = [swap(along[:half], 4), swap(across[half:], 2)]
        corner = jnp.concatenate(corner, axis=0)
        arrived = []
        before = ()
        for i, chunk in enumerate((along, across, corner), 1):
            back, more = expert_block(
                both_cores(after(chunk, back)), raw_blocks[i], grad_blocks[i], mine_blocks[i], before
            )
            mores.append(more)
            part = pair_sum(back)
            before = (part,)
            arrived.append(swap(part, CHIPS[i]))
        grad_gate = sum_over([contract_rows(more[2], more[0]) for more in mores])
        grad_up = sum_over([contract_rows(more[3], more[0]) for more in mores])
        arrived[-1], grad_gate, grad_up = lax.optimization_barrier((arrived[-1], grad_gate, grad_up))
        back_sum = add_parts([pair_sum(own_back), *arrived])
        act_blocks = [more[4] for more in mores]
    else:
        rounds = max(1, dp_count // 8)
        size = group_rows // rounds
        rounds_weights = weights_all.reshape(dp_count, rounds, size, local_experts)
        backs = []
        for i in range(rounds):
            rows = (hidden_line[i * size : (i + 1) * size], grad_line[i * size : (i + 1) * size])
            if backs:
                rows = after(rows, backs[-1], sums)
            hidden, grad = (gather_plane(r) for r in rows)
            mine = rounds_weights[:, i].reshape(-1, local_experts)
            back, more = expert_block(hidden, against_rows(grad, cat_down), grad, mine)
            sums = weight_grads(sums, more)
            act_blocks.append(more[4])
            backs.append(scatter_plane(back))
        back_sum = jnp.concatenate(backs, axis=0)
    d_hidden_mid = scatter_rows(back_sum)

    if four_chips():
        out_products = [as_half(product(act, cat_down)) for act in after(act_blocks, back_sum)]
        d_hidden_mid, out_products = lax.optimization_barrier((d_hidden_mid, out_products))
    grad_gain_ffn = jnp.sum(d_hidden_mid * normed_mid, axis=0)
    d_mid = out_grad + norm_back(d_hidden_mid, normed_mid, scale_mid, gain_ffn)
    mid_low = as_half(d_mid)
    act_blocks = after(act_blocks, back_sum)
    if four_chips():
        out_parts = [pair_sum(out) for out in out_products]
    else:
        for act in act_blocks:
            if out_parts:
                act = after(act, out_parts[-1])
            out_parts.append(scatter_plane(as_half(product(act, cat_down))))

    mid_all = gather_rows(mid_low)
    if four_chips():
        late_acts = after(act_blocks, mid_low)
        grad_down = sum_over([contract_rows(a, g) for a, g in zip(late_acts, grad_blocks)])
        sums = (grad_gate, grad_up, grad_down)
    mid_all = after(mid_all, sums)
    first_shared = local_experts * expert_units
    share = shared_units[0].shape[0]
    shared_sums = [as_half(g[first_shared : first_shared + share]) for g in sums]
    grad_proj_out = contract_rows(mid_all, attended)
    d_attended = product(mid_all, proj_out)
    d_attended = as_half(d_attended).reshape(group_rows, heads, VDIM)
    scale = 1.0 / math.sqrt(NOPE + ROPE)
    scores = score_block(query_nope, query_rope, key_nope, rope_all, mask)
    probs = jnp.exp(scores - total[..., None])
    probs_low = as_half(probs)
    value_grads = jnp.einsum(
        "hqk,qhd->khd", probs_low, d_attended, preferred_element_type=jnp.float32
    )
    d_probs = jnp.einsum("qhd,khd->hqk", d_attended, values, preferred_element_type=jnp.float32)
    delta = jnp.sum(probs * d_probs, axis=-1, keepdims=True)
    d_scores = as_half(probs * (d_probs - delta) * scale)
    query_nope_grads = jnp.einsum(
        "hqk,khd->qhd", d_scores, key_nope, preferred_element_type=jnp.float32
    )
    query_rope_grads = jnp.einsum(
        "hqk,kd->qhd", d_scores, rope_all, preferred_element_type=jnp.float32
    )
    key_nope_grads = jnp.einsum(
        "hqk,qhd->khd", d_scores, query_nope, preferred_element_type=jnp.float32
    )
    rope_key_grads = jnp.einsum(
        "hqk,qhd->kd", d_scores, query_rope, preferred_element_type=jnp.float32
    )
    d_query_rope = unrotate(query_rope_grads, cos_all[:, None, :], sin_all[:, None, :])
    d_query = as_half(jnp.concatenate([query_nope_grads, d_query_rope], axis=-1)).reshape(
        group_rows, heads * (NOPE + ROPE)
    )
    grad_up_q = contract_rows(query_all, d_query)
    d_query_latent = against_rows(d_query, up_q)
    d_key_value = as_half(jnp.concatenate([key_nope_grads, value_grads], axis=-1)).reshape(
        group_rows, heads * (NOPE + VDIM)
    )
    grad_up_kv = contract_rows(key_all, d_key_value)
    d_key_latent = against_rows(d_key_value, up_kv)
    d_latents_own = jnp.concatenate(
        [as_half(d_query_latent), as_half(d_key_latent), as_half(rope_key_grads)], axis=1
    )
    shared_grads = join_units(after(shared_sums, d_latents_own))
    d_latents = scatter_rows(d_latents_own)
    d_latents, shared_grads = lax.optimization_barrier((d_latents, shared_grads))
    sums = after(sums, d_latents_own)
    grad_gate, grad_up, grad_down = sums

    def fold_whole(grads, index):
        width = denses[index].shape[1]
        part = as_half(grads).reshape(dp_count, times[index], base, width).transpose(0, 2, 1, 3)
        return part.reshape(dp_count * base, -1)

    dense_grads = (grad_up_q, grad_up_kv, grad_proj_out)
    folded_grads = jnp.concatenate([fold_whole(g, i) for i, g in enumerate(dense_grads)], axis=1)
    folded_grads = after(folded_grads, d_latents_own)
    if four_chips():
        dense_own = parts_of(reorder(folded_grads, 0))
        dense_parts = [send_part(p, m) for p, m in zip(dense_own, CHIPS)]
        out_parts = [send_part(p, m) for p, m in zip(out_parts, CHIPS)]
        out_sum = add_parts(out_parts)
    else:
        dense_sums = scatter_plane(folded_grads)
        out_sum = jnp.concatenate(out_parts, axis=0)
    block_output = mid + scatter_rows(after(out_sum, d_latents_own))
    latent_q = d_latents[:, :q_rank]
    latent_k = d_latents[:, q_rank : q_rank + KVRANK]
    latent_r = d_latents[:, q_rank + KVRANK :]
    grad_gain_query = jnp.sum(latent_q * normed_query, axis=0)
    d_query_raw = norm_back(latent_q, normed_query, scale_query, gain_query)
    grad_gain_key = jnp.sum(latent_k * normed_key, axis=0)
    d_key_raw = norm_back(latent_k, normed_key, scale_key, gain_key)
    d_rope_raw = unrotate(latent_r, cos_own, sin_own)
    extra = packed.shape[1] - raw_width
    d_raw = as_half(
        jnp.concatenate(
            [d_query_raw, d_key_raw, d_rope_raw, jnp.zeros((own_rows, extra), jnp.float32)], axis=1
        )
    )
    d_hidden_in = against_rows(d_raw, packed)
    grad_gain_attn = jnp.sum(d_hidden_in * normed_in, axis=0)
    input_grad = d_mid + reorder(norm_back(d_hidden_in, normed_in, scale_in, gain_attn), 1)
    rank_grads = jnp.concatenate(
        [grad_gain_query.reshape(-1, q_shard), grad_gain_key.reshape(-1, shard - q_shard)], axis=1
    ).reshape(-1)
    late_grads = reorder(jnp.stack([grad_gain_ffn, rank_grads]), 1)
    gain_grads = jnp.concatenate([grad_gain_attn[None], late_grads], axis=0).T
    packed_grads = contract_rows(hidden_in, d_raw)
    packed_grads = packed_grads + jnp.pad(gain_grads, ((0, 0), (raw_width, 0)))
    if four_chips():
        packed_parts = [send_part(p, m) for p, m in zip(parts_of(as_half(packed_grads)), CHIPS)]
        packed_sums = add_parts(packed_parts)
        dense_sums = add_parts(after(dense_parts, packed_sums))
    else:
        packed_sums = scatter_plane(as_half(packed_grads))
    down_out = scatter_rows(packed_sums)
    up_q_out, up_kv_out, proj_grad_out = (
        as_single(unfold_rows(dense_sums[:, ends[i] : ends[i + 1]], times[i])) for i in range(3)
    )
    grad_gate_sh, grad_up_sh, grad_down_sh = (as_single(g) for g in shared_grads)
    gains_out = down_out[:, raw_width:]

    routed_units = local_experts * expert_units

    def cut(grads):
        return grads[:routed_units].reshape(local_experts, expert_units, model).swapaxes(1, 2)

    return (
        block_output,
        input_grad,
        gains_out[:, 0],
        down_out[:, :q_rank],
        gains_out[:q_shard, 2],
        up_q_out,
        down_out[:, q_rank:raw_width],
        gains_out[q_shard:, 2],
        up_kv_out,
        proj_grad_out,
        gains_out[:, 1],
        grad_gate_sh,
        grad_up_sh,
        grad_down_sh,
        cut(grad_gate),
        cut(grad_up),
        cut(grad_down),
    )


def solution(mesh):
    in_specs = (
        P(("dp", "tensor"), None),
        P(("dp", "tensor"), None),
        P("dp"),
        P("dp", None),
        P("dp", None),
        P(("dp", "tensor")),
        P(("dp", "tensor"), None),
        P(("dp", "tensor")),
        P("dp", "tensor"),
        P(("dp", "tensor"), None),
        P(("dp", "tensor")),
        P("dp", "tensor"),
        P("dp", "tensor"),
        P(("dp", "tensor")),
        P("dp", "tensor"),
        P("dp", "tensor"),
        P("dp", "tensor"),
        P("dp", None, "tensor"),
        P("dp", None, "tensor"),
        P("dp", None, "tensor"),
    )
    out_specs = (
        P(("dp", "tensor"), None),
        P(("dp", "tensor"), None),
        P(("dp", "tensor")),
        P(("dp", "tensor"), None),
        P(("dp", "tensor")),
        P("dp", "tensor"),
        P(("dp", "tensor"), None),
        P(("dp", "tensor")),
        P("dp", "tensor"),
        P("dp", "tensor"),
        P(("dp", "tensor")),
        P("dp", "tensor"),
        P("dp", "tensor"),
        P("dp", "tensor"),
        P("dp", None, "tensor"),
        P("dp", None, "tensor"),
        P("dp", None, "tensor"),
    )
    return jax.shard_map(layer, mesh=mesh, in_specs=in_specs, out_specs=out_specs, check_vma=False)
```

```python
import math

import jax
import jax.numpy as jnp
from jax import lax
from jax.experimental.layout import Layout, with_layout_constraint
from jax.sharding import PartitionSpec as P

NOPE = 128
ROPE = 64
VDIM = 128
KVRANK = 512
SEQ = 512


EPS = 1e-06
THETA = 50000.0


def as_half(values):
    return values.astype(jnp.bfloat16)


def as_single(values):
    return values.astype(jnp.float32)


def product(left, right):
    return jnp.dot(left, right, preferred_element_type=jnp.float32)


def contract_rows(left, right):
    return lax.dot_general(
        left, right, (((0,), (0,)), ((), ())), preferred_element_type=jnp.float32
    )


def against_rows(left, right):
    return lax.dot_general(
        left, right, (((1,), (1,)), ((), ())), preferred_element_type=jnp.float32
    )


def rms_scale(values):
    return lax.rsqrt(jnp.mean(values * values, axis=-1, keepdims=True) + EPS)


def norm_back(grad, normed, scale, gain):
    scaled = grad * gain
    return scale * (scaled - normed * jnp.mean(scaled * normed, axis=-1, keepdims=True))


def angles(positions):
    half = ROPE // 2
    freq = THETA ** (-jnp.arange(half, dtype=jnp.float32) * 2.0 / ROPE)
    phase = as_single(positions)[:, None] * freq[None, :]
    return (jnp.cos(phase), jnp.sin(phase))


def rotate(values, cosine, sine):
    half = values.shape[-1] // 2
    first = values[..., :half]
    second = values[..., half:]
    return jnp.concatenate(
        [first * cosine - second * sine, second * cosine + first * sine], axis=-1
    )


def unrotate(values, cosine, sine):
    half = values.shape[-1] // 2
    first = values[..., :half]
    second = values[..., half:]
    return jnp.concatenate(
        [first * cosine + second * sine, second * cosine - first * sine], axis=-1
    )


def score_block(query_nope, query_rope, key_nope, rope_key, mask):
    scale = 1.0 / math.sqrt(NOPE + ROPE)
    scores = jnp.einsum("qhd,khd->hqk", query_nope, key_nope, preferred_element_type=jnp.float32)
    scores = scores + jnp.einsum(
        "qhd,kd->hqk", query_rope, rope_key, preferred_element_type=jnp.float32
    )
    return jnp.where(mask[None], scores * scale, -jnp.inf)


def after(value, *before):
    return lax.optimization_barrier((value, before))[0]


def fold_rows(rows, base):
    _, width = rows.shape
    return rows.reshape(-1, base, width).transpose(1, 0, 2).reshape(base, -1)


def unfold_rows(rows, times):
    base = rows.shape[0]
    return rows.reshape(base, times, -1).transpose(1, 0, 2).reshape(base * times, -1)


def swap(rows, mask):
    count = lax.axis_size("dp")
    return lax.ppermute(rows, "dp", [(i, i ^ mask) for i in range(count)])


def four_chips():
    return lax.axis_size("dp") == 2 * 2 * 2


def fetch_chunks(rows):
    half = rows.shape[0] // 2
    along = swap(rows, 2)
    across = swap(rows, 4)
    side = swap(rows, 1)
    first = swap(along[:half], 4)
    second = swap(across[half:], 2)
    corner = jnp.concatenate([first, second], axis=0)
    return {
        0: rows,
        1: side,
        2: along,
        3: swap(along, 1),
        4: across,
        5: swap(across, 1),
        6: corner,
        7: swap(corner, 1),
    }


CHIPS = (0, 2, 4, 6)


def both_cores(rows):
    return jnp.concatenate([rows, swap(rows, 1)], axis=0)


def pair_sum(block):
    count = block.shape[0] // 2
    return as_half(as_single(block[:count]) + as_single(swap(block[count:], 1)))


def send_part(part, mask):
    return swap(part, mask) if mask else part


def add_parts(parts):
    total = as_single(parts[0])
    for part in parts[1:]:
        total = total + as_single(part)
    return as_half(total)


def scatter_plane(block):
    return lax.psum_scatter(block, "dp", scatter_dimension=0, tiled=True)


def gather_plane(block):
    return lax.all_gather(block, "dp", axis=0, tiled=True)


def row_major(values):
    return with_layout_constraint(values, Layout(major_to_minor=(0, 1)))


def fetch_list(rows):
    if not four_chips():
        return [lax.all_gather(rows, "dp", axis=0, tiled=True)]
    chunks = fetch_chunks(rows)
    return [chunks[m] for m in range(len(chunks))]


def assemble(chunks):
    if len(chunks) == 1:
        return chunks[0]
    place = lax.axis_index("dp")
    count, width = chunks[0].shape
    whole = jnp.zeros((count * len(chunks), width), chunks[0].dtype)
    for mask, chunk in enumerate(chunks):
        whole = lax.dynamic_update_slice(whole, chunk, ((place ^ mask) * count, 0))
    return row_major(whole)


def reorder(values, axis):
    if not four_chips():
        return values
    place = lax.axis_index("dp")
    count = lax.axis_size("dp")
    size = values.shape[axis] // count
    return jnp.concatenate(
        [
            lax.dynamic_slice_in_dim(values, (place ^ m) * size, size, axis=axis)
            for m in range(count)
        ],
        axis=axis,
    )


def parts_of(rows):
    count = rows.shape[0] // lax.axis_size("dp")

    def part(mask):
        return rows[mask * count : (mask + 1) * count]

    return [
        as_half(as_single(part(m)) + as_single(swap(part(m | 1), 1))) for m in CHIPS
    ]


def gather_rows(rows):
    return lax.all_gather(rows, "tensor", axis=0, tiled=True)


def scatter_rows(rows):
    return as_single(
        lax.psum_scatter(as_half(rows), "tensor", scatter_dimension=0, tiled=True)
    )


def exchange(block):
    return lax.all_to_all(block, "dp", split_axis=0, concat_axis=0, tiled=True)


def split_units(weights):
    dp_count = lax.axis_size("dp")
    rows, units = weights[0].shape
    share = units // dp_count
    stacked = jnp.stack([w.T for w in weights]).reshape(3, dp_count, share, rows)
    stacked = stacked.transpose(1, 0, 2, 3).reshape(dp_count, 3 * share, rows)
    got = exchange(stacked).reshape(dp_count, 3, share, rows)
    return got.transpose(1, 2, 0, 3).reshape(3, share, dp_count * rows)


def join_units(grads):
    dp_count = lax.axis_size("dp")
    share, all_rows = grads[0].shape
    rows = all_rows // dp_count
    stacked = jnp.stack(grads).reshape(3, share, dp_count, rows).transpose(2, 0, 1, 3)
    got = exchange(stacked.reshape(dp_count, 3 * share, rows)).reshape(dp_count, 3, share, rows)
    return [g.T for g in got.transpose(1, 0, 2, 3).reshape(3, dp_count * share, rows)]


def pad_rows(rows):
    return jnp.pad(rows, ((0, -rows.shape[0] % 16), (0, 0)))


def join_rows(experts_weight, shared_slice):
    count, model, units = experts_weight.shape
    return jnp.concatenate(
        [experts_weight.swapaxes(1, 2).reshape(count * units, model), shared_slice], axis=0
    )


def layer(
    block_input,
    out_grad,
    segments,
    routes,
    route_weight,
    norm_attn,
    query_down,
    query_norm,
    query_up,
    latent_down,
    latent_norm,
    latent_up,
    out_proj,
    norm_ffn,
    shared_gate,
    shared_up,
    shared_down,
    expert_gate,
    expert_up,
    expert_down,
):
    dp_count = lax.axis_size("dp")
    place = lax.axis_index("dp")
    quarter = lax.axis_index("tensor")
    own_rows = block_input.shape[0]
    group_rows = segments.shape[0]
    local_experts, model, expert_units = expert_gate.shape
    experts = local_experts * dp_count
    q_rank = query_down.shape[1]
    raw_width = q_rank + latent_down.shape[1]
    shard = query_down.shape[0]
    q_shard = query_norm.shape[0]

    packed_own = jnp.concatenate(
        [
            query_down,
            latent_down,
            norm_attn[:, None],
            norm_ffn[:, None],
            jnp.concatenate([query_norm, latent_norm])[:, None],
        ],
        axis=1,
    )
    packed_line = gather_rows(packed_own)
    base = latent_up.shape[0]
    denses = (query_up, latent_up, out_proj)
    times = [w.shape[0] // base for w in denses]
    ends = [0]
    for w in denses:
        ends.append(ends[-1] + w.size // base)
    chosen = routes[:, :, None] == jnp.arange(experts, dtype=jnp.int32)[None, None, :]
    dense_weight = jnp.sum(jnp.where(chosen, route_weight[:, :, None], 0.0), axis=1)
    upper = as_half(dense_weight)
    terms = jnp.concatenate([upper, as_half(dense_weight - as_single(upper))], axis=1)
    folds = [fold_rows(w, base) for w in (*denses, terms)]
    folded_chunks = fetch_list(jnp.concatenate(after(folds, packed_own), axis=1))

    def unfold_whole(index):
        part = folded[:, ends[index] : ends[index + 1]]
        width = denses[index].shape[1]
        part = part.reshape(dp_count, base, times[index], width).transpose(0, 2, 1, 3)
        return part.reshape(-1, width)

    packed_line, folded_chunks = lax.optimization_barrier((packed_line, folded_chunks))
    packed_chunks = fetch_list(row_major(packed_line))
    folded = assemble(folded_chunks)
    up_q, up_kv, proj_out = (unfold_whole(i) for i in range(3))
    terms_all = folded[:, ends[3] :].reshape(dp_count, base, group_rows // base, 2, experts)
    mine_terms = lax.dynamic_slice_in_dim(terms_all, place * local_experts, local_experts, axis=4)
    mine_terms = as_single(mine_terms).transpose(0, 2, 1, 3, 4)
    weights_all = jnp.sum(mine_terms, axis=3).reshape(-1, local_experts)
    grad_line = gather_rows(after(as_half(out_grad), packed_line))
    grad_sent = after(grad_line, packed_chunks)
    shared_units = split_units(after([shared_gate, shared_up, shared_down], packed_chunks))
    if four_chips():
        grad_chunks = [grad_sent] + [swap(grad_sent, m) for m in CHIPS[1:]]

    scale_in = rms_scale(block_input)
    normed_in = reorder(block_input * scale_in, 1)
    raw = None
    hidden_pieces = []
    gain_pieces = []
    for i, chunk in enumerate(packed_chunks):
        size = chunk.shape[0]
        normed_piece = normed_in[:, i * size : (i + 1) * size]
        chunk, normed_piece = lax.optimization_barrier((chunk, normed_piece))
        piece_gains = as_single(chunk[:, raw_width:]).T
        piece = as_half(normed_piece * piece_gains[0])
        more = product(piece, chunk)
        raw = more if raw is None else raw + more
        hidden_pieces.append(piece)
        gain_pieces.append(piece_gains)
    late_gains = gain_pieces[0][1:]
    if four_chips():
        late_gains = jnp.zeros((2, model), jnp.float32)
        for mask, piece_gains in enumerate(gain_pieces):
            late_gains = lax.dynamic_update_slice(
                late_gains, piece_gains[1:], (0, (place ^ mask) * piece_gains.shape[1])
            )
    gain_ffn, rank_gains = late_gains
    rank_gains = rank_gains.reshape(-1, shard)
    gain_query = rank_gains[:, :q_shard].reshape(-1)
    gain_key = rank_gains[:, q_shard:].reshape(-1)
    query_raw = raw[:, :q_rank]
    scale_query = rms_scale(query_raw)
    normed_query = query_raw * scale_query
    query_latent = as_half(normed_query * gain_query)
    key_raw = raw[:, q_rank : q_rank + KVRANK]
    scale_key = rms_scale(key_raw)
    normed_key = key_raw * scale_key
    key_latent = as_half(normed_key * gain_key)
    own_positions = (quarter * own_rows + jnp.arange(own_rows, dtype=jnp.int32)) % SEQ
    cos_own, sin_own = angles(own_positions)
    rope_own = as_half(rotate(raw[:, q_rank + KVRANK : raw_width], cos_own, sin_own))
    latents_own = jnp.concatenate([query_latent, key_latent, rope_own], axis=1)
    latents = gather_rows(after(latents_own, grad_line))
    hidden_in = jnp.concatenate(after(hidden_pieces, latents_own), axis=1)
    query_all = latents[:, :q_rank]
    key_all = latents[:, q_rank : q_rank + KVRANK]
    rope_all = latents[:, q_rank + KVRANK :]
    heads = up_q.shape[1] // (NOPE + ROPE)
    cos_all, sin_all = angles(jnp.arange(group_rows, dtype=jnp.int32) % SEQ)
    query_full = product(query_all, up_q).reshape(group_rows, heads, NOPE + ROPE)
    query_nope = as_half(query_full[..., :NOPE])
    query_rope = as_half(rotate(query_full[..., NOPE:], cos_all[:, None, :], sin_all[:, None, :]))
    key_value = as_half(product(key_all, up_kv)).reshape(group_rows, heads, NOPE + VDIM)
    key_nope = key_value[..., :NOPE]
    values = key_value[..., NOPE:]
    places = jnp.arange(SEQ, dtype=jnp.int32)
    causal = places[:, None] >= places[None, :]
    mask = causal & (segments[:, None] == segments[None, :])
    scores = score_block(query_nope, query_rope, key_nope, rope_all, mask)
    total = jax.nn.logsumexp(scores, axis=-1)
    probs = as_half(jnp.exp(scores - total[..., None]))
    mixed = jnp.einsum("hqk,khd->qhd", probs, values, preferred_element_type=jnp.float32)
    attended = as_half(mixed).reshape(group_rows, heads * VDIM)
    projected = against_rows(attended, proj_out)
    mid = block_input + scatter_rows(projected)
    sg, su, sd = (pad_rows(w) for w in after(shared_units, projected))
    cat_gate = join_rows(expert_gate, sg)
    cat_up = join_rows(expert_up, su)
    cat_down = join_rows(expert_down, sd)
    cat_both = jnp.concatenate([cat_gate, cat_up], axis=0)
    column = jnp.arange(cat_gate.shape[0])[None, :]
    scale_mid = rms_scale(mid)
    normed_mid = mid * scale_mid
    hidden_mid = as_half(normed_mid * gain_ffn)

    hidden_line = gather_rows(hidden_mid)

    def expert_block(hidden, d_act_raw, grad, mine, before=()):
        factor = jnp.ones((1, 1), jnp.float32)
        for e in range(local_experts):
            inside = (column >= e * expert_units) & (column < (e + 1) * expert_units)
            factor = jnp.where(inside, mine[:, e : e + 1], factor)
        gate_val = against_rows(hidden, cat_gate)
        hidden, gate_val = after((hidden, gate_val), before)
        up_val = against_rows(hidden, cat_up)
        d_act = d_act_raw * factor
        sigma = jax.nn.sigmoid(gate_val)
        act = as_half(gate_val * sigma * up_val)
        act = as_half(as_single(act) * factor)
        d_gate = as_half(d_act * up_val * sigma * (1.0 + gate_val * (1.0 - sigma)))
        d_up = as_half(d_act * gate_val * sigma)
        back = product(jnp.concatenate([d_gate, d_up], axis=1), cat_both)
        back = as_half(back)
        more = (hidden, grad, d_gate, d_up, act)
        return back, more

    def weight_grads(sums, more):
        hidden, grad, d_gate, d_up, act = more
        new = (
            contract_rows(d_gate, hidden),
            contract_rows(d_up, hidden),
            contract_rows(act, grad),
        )
        return new if sums is None else tuple(x + y for x, y in zip(sums, new))

    def sum_over(terms):
        total = terms[0]
        for term in terms[1:]:
            total = total + term
        return total

    sums = None
    act_blocks = []
    out_parts = []
    if four_chips():
        def block_weights(mask):
            far = [
                lax.dynamic_slice_in_dim(weights_all, (place ^ m) * group_rows, group_rows, axis=0)
                for m in (mask, mask | 1)
            ]
            return jnp.concatenate(far, axis=0)

        grad_chunks = after(grad_chunks, projected)
        grad_blocks = [both_cores(chunk) for chunk in grad_chunks]
        raw_blocks = [against_rows(grad, cat_down) for grad in grad_blocks]
        mine_blocks = [block_weights(m) for m in CHIPS]
        hidden_line, raw_blocks, mine_blocks = lax.optimization_barrier(
            (hidden_line, raw_blocks, mine_blocks)
        )
        half = group_rows // 2
        along = swap(hidden_line, 2)
        across = swap(hidden_line, 4)
        back, more = expert_block(
            both_cores(hidden_line), raw_blocks[0], grad_blocks[0], mine_blocks[0]
        )
        mores = [more]
        own_back = back
        along, across = after((along, across), back)
        corner = [swap(along[:half], 4), swap(across[half:], 2)]
        corner = jnp.concatenate(corner, axis=0)
        arrived = []
        before = ()
        for i, chunk in enumerate((along, across, corner), 1):
            back, more = expert_block(
                both_cores(after(chunk, back)), raw_blocks[i], grad_blocks[i], mine_blocks[i], before
            )
            mores.append(more)
            part = pair_sum(back)
            before = (part,)
            arrived.append(swap(part, CHIPS[i]))
        grad_gate = sum_over([contract_rows(more[2], more[0]) for more in mores])
        grad_up = sum_over([contract_rows(more[3], more[0]) for more in mores])
        arrived[-1], grad_gate, grad_up = lax.optimization_barrier((arrived[-1], grad_gate, grad_up))
        back_sum = add_parts([pair_sum(own_back), *arrived])
        act_blocks = [more[4] for more in mores]
    else:
        rounds = max(1, dp_count // 8)
        size = group_rows // rounds
        rounds_weights = weights_all.reshape(dp_count, rounds, size, local_experts)
        backs = []
        for i in range(rounds):
            rows = (hidden_line[i * size : (i + 1) * size], grad_line[i * size : (i + 1) * size])
            if backs:
                rows = after(rows, backs[-1], sums)
            hidden, grad = (gather_plane(r) for r in rows)
            mine = rounds_weights[:, i].reshape(-1, local_experts)
            back, more = expert_block(hidden, against_rows(grad, cat_down), grad, mine)
            sums = weight_grads(sums, more)
            act_blocks.append(more[4])
            backs.append(scatter_plane(back))
        back_sum = jnp.concatenate(backs, axis=0)
    d_hidden_mid = scatter_rows(back_sum)

    if four_chips():
        out_products = [as_half(product(act, cat_down)) for act in after(act_blocks, back_sum)]
        d_hidden_mid, out_products = lax.optimization_barrier((d_hidden_mid, out_products))
    grad_gain_ffn = jnp.sum(d_hidden_mid * normed_mid, axis=0)
    d_mid = out_grad + norm_back(d_hidden_mid, normed_mid, scale_mid, gain_ffn)
    mid_low = as_half(d_mid)
    act_blocks = after(act_blocks, back_sum)
    if four_chips():
        out_parts = [pair_sum(out) for out in out_products]
    else:
        for act in act_blocks:
            if out_parts:
                act = after(act, out_parts[-1])
            out_parts.append(scatter_plane(as_half(product(act, cat_down))))

    mid_all = gather_rows(mid_low)
    if four_chips():
        late_acts = after(act_blocks, mid_low)
        grad_down = sum_over([contract_rows(a, g) for a, g in zip(late_acts, grad_blocks)])
        sums = (grad_gate, grad_up, grad_down)
    mid_all = after(mid_all, sums)
    first_shared = local_experts * expert_units
    share = shared_units[0].shape[0]
    shared_sums = [as_half(g[first_shared : first_shared + share]) for g in sums]
    grad_proj_out = contract_rows(mid_all, attended)
    d_attended = product(mid_all, proj_out)
    d_attended = as_half(d_attended).reshape(group_rows, heads, VDIM)
    scale = 1.0 / math.sqrt(NOPE + ROPE)
    scores = score_block(query_nope, query_rope, key_nope, rope_all, mask)
    probs = jnp.exp(scores - total[..., None])
    probs_low = as_half(probs)
    value_grads = jnp.einsum(
        "hqk,qhd->khd", probs_low, d_attended, preferred_element_type=jnp.float32
    )
    d_probs = jnp.einsum("qhd,khd->hqk", d_attended, values, preferred_element_type=jnp.float32)
    delta = jnp.sum(probs * d_probs, axis=-1, keepdims=True)
    d_scores = as_half(probs * (d_probs - delta) * scale)
    query_nope_grads = jnp.einsum(
        "hqk,khd->qhd", d_scores, key_nope, preferred_element_type=jnp.float32
    )
    query_rope_grads = jnp.einsum(
        "hqk,kd->qhd", d_scores, rope_all, preferred_element_type=jnp.float32
    )
    key_nope_grads = jnp.einsum(
        "hqk,qhd->khd", d_scores, query_nope, preferred_element_type=jnp.float32
    )
    rope_key_grads = jnp.einsum(
        "hqk,qhd->kd", d_scores, query_rope, preferred_element_type=jnp.float32
    )
    d_query_rope = unrotate(query_rope_grads, cos_all[:, None, :], sin_all[:, None, :])
    d_query = as_half(jnp.concatenate([query_nope_grads, d_query_rope], axis=-1)).reshape(
        group_rows, heads * (NOPE + ROPE)
    )
    grad_up_q = contract_rows(query_all, d_query)
    d_query_latent = against_rows(d_query, up_q)
    d_key_value = as_half(jnp.concatenate([key_nope_grads, value_grads], axis=-1)).reshape(
        group_rows, heads * (NOPE + VDIM)
    )
    grad_up_kv = contract_rows(key_all, d_key_value)
    d_key_latent = against_rows(d_key_value, up_kv)
    d_latents_own = jnp.concatenate(
        [as_half(d_query_latent), as_half(d_key_latent), as_half(rope_key_grads)], axis=1
    )
    shared_grads = join_units(after(shared_sums, d_latents_own))
    d_latents = scatter_rows(d_latents_own)
    d_latents, shared_grads = lax.optimization_barrier((d_latents, shared_grads))
    sums = after(sums, d_latents_own)
    grad_gate, grad_up, grad_down = sums

    def fold_whole(grads, index):
        width = denses[index].shape[1]
        part = as_half(grads).reshape(dp_count, times[index], base, width).transpose(0, 2, 1, 3)
        return part.reshape(dp_count * base, -1)

    dense_grads = (grad_up_q, grad_up_kv, grad_proj_out)
    folded_grads = jnp.concatenate([fold_whole(g, i) for i, g in enumerate(dense_grads)], axis=1)
    folded_grads = after(folded_grads, d_latents_own)
    if four_chips():
        dense_own = parts_of(reorder(folded_grads, 0))
        dense_parts = [send_part(p, m) for p, m in zip(dense_own, CHIPS)]
        out_parts = [send_part(p, m) for p, m in zip(out_parts, CHIPS)]
        out_sum = add_parts(out_parts)
    else:
        dense_sums = scatter_plane(folded_grads)
        out_sum = jnp.concatenate(out_parts, axis=0)
    block_output = mid + scatter_rows(after(out_sum, d_latents_own))
    latent_q = d_latents[:, :q_rank]
    latent_k = d_latents[:, q_rank : q_rank + KVRANK]
    latent_r = d_latents[:, q_rank + KVRANK :]
    grad_gain_query = jnp.sum(latent_q * normed_query, axis=0)
    d_query_raw = norm_back(latent_q, normed_query, scale_query, gain_query)
    grad_gain_key = jnp.sum(latent_k * normed_key, axis=0)
    d_key_raw = norm_back(latent_k, normed_key, scale_key, gain_key)
    d_rope_raw = unrotate(latent_r, cos_own, sin_own)
    extra = packed_own.shape[1] - raw_width
    d_raw = as_half(
        jnp.concatenate(
            [d_query_raw, d_key_raw, d_rope_raw, jnp.zeros((own_rows, extra), jnp.float32)], axis=1
        )
    )
    d_hidden_in = jnp.concatenate([against_rows(d_raw, c) for c in packed_chunks], axis=1)
    scaled_in = jnp.concatenate(
        [against_rows(d_raw, c) * g[0] for c, g in zip(packed_chunks, gain_pieces)], axis=1
    )
    grad_gain_attn = jnp.sum(d_hidden_in * normed_in, axis=0)
    inner = jnp.mean(scaled_in * normed_in, axis=-1, keepdims=True)
    input_grad = d_mid + reorder(scale_in * (scaled_in - normed_in * inner), 1)
    rank_grads = jnp.concatenate(
        [grad_gain_query.reshape(-1, q_shard), grad_gain_key.reshape(-1, shard - q_shard)], axis=1
    ).reshape(-1)
    late_grads = reorder(jnp.stack([grad_gain_ffn, rank_grads]), 1)
    gain_grads = jnp.concatenate([grad_gain_attn[None], late_grads], axis=0).T
    packed_grads = contract_rows(hidden_in, d_raw)
    packed_grads = packed_grads + jnp.pad(gain_grads, ((0, 0), (raw_width, 0)))
    if four_chips():
        packed_parts = [send_part(p, m) for p, m in zip(parts_of(as_half(packed_grads)), CHIPS)]
        packed_sums = add_parts(packed_parts)
        dense_sums = add_parts(after(dense_parts, packed_sums))
    else:
        packed_sums = scatter_plane(as_half(packed_grads))
    down_out = scatter_rows(packed_sums)
    up_q_out, up_kv_out, proj_grad_out = (
        as_single(unfold_rows(dense_sums[:, ends[i] : ends[i + 1]], times[i])) for i in range(3)
    )
    grad_gate_sh, grad_up_sh, grad_down_sh = (as_single(g) for g in shared_grads)
    gains_out = down_out[:, raw_width:]

    routed_units = local_experts * expert_units

    def cut(grads):
        return grads[:routed_units].reshape(local_experts, expert_units, model).swapaxes(1, 2)

    return (
        block_output,
        input_grad,
        gains_out[:, 0],
        down_out[:, :q_rank],
        gains_out[:q_shard, 2],
        up_q_out,
        down_out[:, q_rank:raw_width],
        gains_out[q_shard:, 2],
        up_kv_out,
        proj_grad_out,
        gains_out[:, 1],
        grad_gate_sh,
        grad_up_sh,
        grad_down_sh,
        cut(grad_gate),
        cut(grad_up),
        cut(grad_down),
    )


def solution(mesh):
    in_specs = (
        P(("dp", "tensor"), None),
        P(("dp", "tensor"), None),
        P("dp"),
        P("dp", None),
        P("dp", None),
        P(("dp", "tensor")),
        P(("dp", "tensor"), None),
        P(("dp", "tensor")),
        P("dp", "tensor"),
        P(("dp", "tensor"), None),
        P(("dp", "tensor")),
        P("dp", "tensor"),
        P("dp", "tensor"),
        P(("dp", "tensor")),
        P("dp", "tensor"),
        P("dp", "tensor"),
        P("dp", "tensor"),
        P("dp", None, "tensor"),
        P("dp", None, "tensor"),
        P("dp", None, "tensor"),
    )
    out_specs = (
        P(("dp", "tensor"), None),
        P(("dp", "tensor"), None),
        P(("dp", "tensor")),
        P(("dp", "tensor"), None),
        P(("dp", "tensor")),
        P("dp", "tensor"),
        P(("dp", "tensor"), None),
        P(("dp", "tensor")),
        P("dp", "tensor"),
        P("dp", "tensor"),
        P(("dp", "tensor")),
        P("dp", "tensor"),
        P("dp", "tensor"),
        P("dp", "tensor"),
        P("dp", None, "tensor"),
        P("dp", None, "tensor"),
        P("dp", None, "tensor"),
    )
    return jax.shard_map(layer, mesh=mesh, in_specs=in_specs, out_specs=out_specs, check_vma=False)
```
